128 devices in a mesh: depth: 4 (over z), tile: 32 (over x, y, core).
Axes of the slice: x: 4, y: 4, z: 4, core: 2. Of those that a mesh axis runs over, the one named last changes fastest.
Arguments:
- transmission: float32 [2, 8, 8192, 512], P(None, 'depth', 'tile'), may hold values from -0.6 to 1.25, as said below
- probe: float32 [2, 256, 256], replicated, may hold values from -4.2 to 4.2
- intensity: float32 [64, 256, 256], P('tile'), may hold values from 0.25 to 4
- positions: int32 [64, 2], P('tile'), may hold values from 0 to 7936, as said below
- batch: int32 [64], P('tile'), may hold values from 0 to 1
Outputs:
- updated: float32 [2, 8, 8192, 512], P(None, 'depth', 'tile')
The draws below stay inside these ranges and needn't reach their ends.
Inputs may be any that keep to these rules, and one draw needn't show every extreme that they name: `positions`: probe j is held by tile device j // 2; its top row minus 256 times that device's index, plus half of 256, lies between 0 and 255; its left column is at most 256. On every tile device the window of its first probe starts at least 64 rows above the device's rows (unless clipped at the object's top) and the window of its second probe ends at least 64 rows below them (unless clipped at the object's bottom). `transmission`: the first component lies between 0.5 and 1.25, the second between -0.6 and 0.6.
All inputs are finite; a program needn't handle non-finite values.
Results may differ from the reference program's by a relative error of at most 0.0003.
Values sent between devices are 32-bit elements; how exact they have to be, the bound alone decides.
No kernel may reach another device: no remote copies, remote signals or barrier semaphores. Data moves between devices by JAX's collectives and lax.ppermute only.
A program may use at most 192 MiB of HBM per device.

```python
import math
import jax
import jax.numpy as jnp
from jax import lax

PROBE = 256
ROWS_DEV = 256
COLS = 512
PROBES_DEV = 2
SLICES = 8
OBJ_ROWS = 8192
NPROB = 64


def draw_transmission(key, part):
    first, second = jax.random.split(jax.random.fold_in(key, 11))
    shape = (SLICES, OBJ_ROWS, COLS)
    real_part = jax.random.uniform(first, shape, jnp.float32, 0.6, 1.2)
    imag_part = jnp.clip(0.3 * jax.random.normal(second, shape, jnp.float32), -0.6, 0.6)
    return jnp.stack([real_part, imag_part], 0)


def draw_positions(key, part):
    first, second, third, fourth = jax.random.split(jax.random.fold_in(key, 23), 4)
    counter = jnp.arange(NPROB, dtype=jnp.int32)
    owner = counter // PROBES_DEV
    slot = counter % PROBES_DEV
    spread = jax.random.randint(first, (NPROB,), 0, ROWS_DEV, dtype=jnp.int32)
    upper = jax.random.randint(third, (NPROB,), 0, PROBE // 4 + 1, dtype=jnp.int32)
    lower = jax.random.randint(fourth, (NPROB,), ROWS_DEV - PROBE // 4, ROWS_DEV, dtype=jnp.int32)
    offset = jnp.where(slot == 0, upper, jnp.where(slot == 1, lower, spread))
    top_row = jnp.clip(owner * ROWS_DEV - PROBE // 2 + offset, 0, OBJ_ROWS - PROBE)
    left_col = jax.random.randint(second, (NPROB,), 0, COLS - PROBE + 1, dtype=jnp.int32)
    return jnp.stack([top_row, left_col], 1)


def place_ends(entries, stream_key, low, largest):
    longest = entries.shape.index(max(entries.shape))
    spots = []
    for shift in (0, 1):
        where = [jax.random.randint(jax.random.fold_in(stream_key, axis), (), 0, length) for axis, length in enumerate(entries.shape)]
        where[longest] = (where[longest] + shift) % entries.shape[longest]
        spots.append(tuple(where))
    return entries.at[spots[0]].set(low).at[spots[1]].set(largest)


def block_scale(rng, shape, pieces, low, high):
    def one(position, blocks):
        heights = jax.random.uniform(jax.random.fold_in(jax.random.fold_in(rng, 6), position), (blocks,), jnp.float32, low / len(pieces), high / len(pieces))
        return jnp.repeat(jnp.exp(heights), shape[position] // blocks).reshape((-1,) + (1,) * (len(shape) - position - 1))

    factor_of = one(*pieces[0])
    for cut in pieces[1:]:
        factor_of = factor_of * one(*cut)
    return factor_of


def normal_values(own_key, shape, width, reach, kind=jnp.bfloat16):
    entries = jax.random.normal(own_key, shape, jnp.float32) * width
    return jnp.minimum(jnp.maximum(entries, -reach), reach).astype(kind)


def setup_inputs(seed: int = 0) -> dict:
    key_list = jax.random.split(jax.random.key(seed), 6)
    transmission = draw_transmission(jax.random.fold_in(key_list[5], 71), 0)
    probe = normal_values(key_list[1], (2, PROBE, PROBE), 0.7, 4.2, jnp.float32)
    intensity = jnp.clip(jnp.exp(math.log(4.0) - 2.7725887 * jax.random.uniform(key_list[2], (NPROB, PROBE, PROBE), jnp.float32) ** block_scale(key_list[2], (NPROB, PROBE, PROBE), ((0, 32),), -0.2, 0.2)), 0.25, 4.0)
    positions = draw_positions(jax.random.fold_in(key_list[5], 71), 0)
    batch = place_ends(jax.random.randint(key_list[4], (NPROB,), 0, 2), jax.random.fold_in(key_list[4], 1), 0, 1).astype(jnp.int32)
    return {"transmission": transmission, "probe": probe, "intensity": intensity, "positions": positions, "batch": batch}


prop_strength = 24.0
step_rate = 0.08

def left_mul(matrix, field):
    return jnp.einsum('ij,...jk->...ik', matrix, field, precision=lax.Precision.HIGHEST)

def right_mul(field, matrix):
    return jnp.einsum('...ij,jk->...ik', field, matrix, precision=lax.Precision.HIGHEST)

def transform(field, operator_set):
    a_real, a_imag, b_real, b_imag = operator_set
    f_real, f_imag = field
    u_real = left_mul(a_real, f_real) - left_mul(a_imag, f_imag)
    u_imag = left_mul(a_real, f_imag) + left_mul(a_imag, f_real)
    return (right_mul(u_real, b_real) - right_mul(u_imag, b_imag), right_mul(u_real, b_imag) + right_mul(u_imag, b_real))

def product(first, second):
    return (first[0] * second[0] - first[1] * second[1], first[0] * second[1] + first[1] * second[0])

def operators(extent):
    counter = jnp.arange(extent, dtype=jnp.int32)
    phase = counter[:, None] * counter[None, :] % extent
    angles = phase.astype(jnp.float32) * (2.0 * math.pi / extent)
    norming = 1.0 / math.sqrt(extent)
    cosine = jnp.cos(angles) * norming
    sine = jnp.sin(angles) * norming
    freq = jnp.where(counter < extent // 2, counter, counter - extent).astype(jnp.float32) / extent
    turned = -math.pi * prop_strength * freq * freq
    h_real = jnp.cos(turned)
    h_imag = jnp.sin(turned)
    a_real = h_real[:, None] * cosine + h_imag[:, None] * sine
    a_imag = h_imag[:, None] * cosine - h_real[:, None] * sine
    highest = lax.Precision.HIGHEST
    q_real = jnp.dot(cosine, a_real, precision=highest) - jnp.dot(sine, a_imag, precision=highest)
    q_imag = jnp.dot(cosine, a_imag, precision=highest) + jnp.dot(sine, a_real, precision=highest)
    forward = (q_real, q_imag, q_real.T, q_imag.T)
    far_out = (cosine, -sine, cosine, -sine)
    return (forward, far_out)

def probe_loss(obj_patch, probe, measured, weight, forward, far_out):
    wavefront = (probe[0], probe[1])
    for layer in range(obj_patch.shape[1]):
        chi = product((obj_patch[0, layer], obj_patch[1, layer]), wavefront)
        wavefront = transform(chi, forward)
    far = transform(wavefront, far_out)
    resid = far[0] * far[0] + far[1] * far[1] - measured
    return weight * jnp.sum(resid * resid)

def reference(transmission, probe, intensity, positions, batch):
    forward, far_out = operators(PROBE)
    current = transmission
    for turn_at in range(2):

        def visit(grad_sum, number):
            zero = jnp.int32(0)
            start = (zero, zero, positions[number, 0], positions[number, 1])
            obj_patch = lax.dynamic_slice(current, start, (2, SLICES, PROBE, PROBE))
            weight = (batch[number] == turn_at).astype(jnp.float32)
            patch_grad = lax.cond(weight > 0, lambda: jax.grad(probe_loss)(obj_patch, probe, intensity[number], weight, forward, far_out), lambda: jnp.zeros_like(obj_patch))
            region = lax.dynamic_slice(grad_sum, start, (2, SLICES, PROBE, PROBE)) + patch_grad
            return (lax.dynamic_update_slice(grad_sum, region, start), None)
        grad_sum = lax.scan(visit, jnp.zeros_like(current), jnp.arange(NPROB, dtype=jnp.int32))[0]
        current = current - step_rate * grad_sum
    return current
```

```python
import functools
import math

import jax
import jax.numpy as jnp
import numpy as np
from jax import lax
from jax.experimental import pallas as pl
from jax.experimental.pallas import tpu as pltpu
from jax.sharding import PartitionSpec as P

prop_strength = 24.0
step_rate = 0.08

AXES = ("depth", "tile")
F32 = jnp.float32
BF16 = jnp.bfloat16
CHUNK = 32


def operator_table(extent):
    counter = np.arange(extent)
    angles = 2.0 * np.pi / extent * (counter[:, None] * counter[None, :] % extent)
    far = (np.cos(angles) - 1j * np.sin(angles)) / math.sqrt(extent)
    freq = np.where(counter < extent // 2, counter, counter - extent) / extent
    turned = np.exp(-1j * np.pi * prop_strength * freq * freq)
    near = np.conj(far) @ (turned[:, None] * far)
    parts = []
    for matrix in (near, far):
        for value in (matrix.real, matrix.imag, matrix.real + matrix.imag):
            high = value.astype(BF16)
            low = (value - high.astype(np.float64)).astype(BF16)
            parts += [high, low]
    return np.stack(parts).reshape(2, 3, 2, extent, extent)


def place():
    depth_at = lax.axis_index("depth")
    tile_at = lax.axis_index("tile")
    rel = lax.rem(depth_at + 2 * lax.rem(tile_at, 2), 4)
    return depth_at, tile_at, rel


def split(x):
    high = x.astype(BF16)
    return high, (x - high.astype(F32)).astype(BF16)


def mm(a, b):
    return jnp.dot(a, b, preferred_element_type=F32)


def right_three(x, table, part):
    high, low = split(x)
    return mm(high, table[part, 0]) + (mm(high, table[part, 1]) + mm(low, table[part, 0]))


def left_three(x, table, part):
    high, low = split(x)
    return mm(table[part, 0], high) + (mm(table[part, 1], high) + mm(table[part, 0], low))


def two_sided(x_real, x_imag, table):
    for three in (right_three, left_three):
        first = three(x_real, table, 0)
        second = three(x_imag, table, 1)
        third = three(x_real + x_imag, table, 2)
        x_real, x_imag = first - second, third - first - second
    return x_real, x_imag


def main_kernel(turn_at, batch, probe, intensity, table_in, *rest):
    ins, outs, (obj, seen, wave, measured, table, sems) = rest[:8], rest[8:16], rest[16:]
    layers = 8
    depth_at, tile_at, rel = place()
    slot = lax.rem(rel, 2)
    is_dest = rel < 2
    active = is_dest & (batch[slot] == turn_at)
    near = 1 + 2 * slot
    chunks = [depth_at, lax.rem(depth_at + near, 4), lax.rem(depth_at + 4 - near, 4), lax.rem(depth_at + 2, 4)]
    row_inner = pl.multiple_of(128 * (1 - slot), 128)
    row_halo = pl.multiple_of(128 * slot, 128)

    def half(buffer, number):
        row = row_inner if number < 4 else row_halo
        return buffer.at[chunks[number % 4], :, :, pl.ds(row, 128), :]

    out_copies = [pltpu.make_async_copy(half(seen, n), outs[n], sems.at[n]) for n in range(8)]

    @pl.when(active)
    def _():
        copies = [pltpu.make_async_copy(ins[n], half(obj, n), sems.at[n]) for n in range(8)]
        copies.append(pltpu.make_async_copy(probe, wave, sems.at[8]))
        copies.append(pltpu.make_async_copy(table_in, table, sems.at[9]))
        copies.append(pltpu.make_async_copy(intensity.at[slot], measured, sems.at[10]))
        for copy in copies:
            copy.start()
        for copy in copies:
            copy.wait()

        def forward(k, carry):
            at, s = k // 2, lax.rem(k, 2)
            w_real, w_imag = wave[0], wave[1]
            seen[at, 0, s] = w_real
            seen[at, 1, s] = w_imag
            o_real, o_imag = obj[at, 0, s], obj[at, 1, s]
            wave[0], wave[1] = two_sided(
                o_real * w_real - o_imag * w_imag, o_real * w_imag + o_imag * w_real, table.at[0]
            )
            return carry

        lax.fori_loop(0, layers, forward, 0)
        f_real, f_imag = two_sided(wave[0], wave[1], table.at[1])
        factor = 4.0 * (f_real * f_real + f_imag * f_imag - measured[...])
        wave[0], wave[1] = two_sided(factor * f_real, -(factor * f_imag), table.at[1])

        def backward(step, carry):
            k = layers - 1 - step
            at, s = k // 2, lax.rem(k, 2)
            c_real, c_imag = two_sided(wave[0], wave[1], table.at[0])
            s_real, s_imag = seen[at, 0, s], seen[at, 1, s]
            seen[at, 0, s] = c_real * s_real - c_imag * s_imag
            seen[at, 1, s] = -(c_imag * s_real + c_real * s_imag)
            o_real, o_imag = obj[at, 0, s], obj[at, 1, s]
            wave[0] = o_real * c_real - o_imag * c_imag
            wave[1] = o_real * c_imag + o_imag * c_real
            return carry

        lax.fori_loop(0, layers, backward, 0)

    @pl.when(is_dest & jnp.logical_not(active))
    def _():
        seen[...] = jnp.zeros(seen.shape, F32)

    @pl.when(is_dest)
    def _():
        for copy in out_copies:
            copy.start()
        for copy in out_copies:
            copy.wait()


ANY = pl.BlockSpec(memory_space=pl.ANY)
SMEM = pl.BlockSpec(memory_space=pltpu.SMEM)
HALF = jax.ShapeDtypeStruct((2, 2, 128, 256), F32)


def run_main(turn_at, batch, probe, intensity, table, ins):
    return pl.pallas_call(
        functools.partial(main_kernel, turn_at),
        out_shape=[HALF] * 8,
        in_specs=[SMEM] + [ANY] * 11,
        out_specs=[ANY] * 8,
        scratch_shapes=[
            pltpu.VMEM((4, 2, 2, 256, 256), F32),
            pltpu.VMEM((4, 2, 2, 256, 256), F32),
            pltpu.VMEM((2, 256, 256), F32),
            pltpu.VMEM((256, 256), F32),
            pltpu.VMEM((2, 3, 2, 256, 256), BF16),
            pltpu.SemaphoreType.DMA((11,)),
        ],
        name=f"probe_chain_{turn_at}",
    )(batch, probe, intensity, table, *ins)


def window_offset(positions, slot, tile_at):
    return positions[slot, 0] - 256 * tile_at + 128, positions[slot, 1]


def aligned(row, extent):
    return pl.multiple_of(jnp.minimum(row // 8 * 8, extent - 136), 8)


def cut(source, first_row, col, out):
    turn = lax.rem(512 - col, 512)
    start = aligned(first_row, source.shape[2])
    shift = lax.rem(CHUNK + 8 - (first_row - start), CHUNK + 8)

    def plane(number, carry):
        part, layer = number // 2, lax.rem(number, 2)
        for at in range(0, 128, CHUNK):
            rows = source[part, layer, pl.ds(start + at, CHUNK + 8), :]
            rows = pltpu.roll(rows, shift, 0)[:CHUNK]
            out[part, layer, pl.ds(at, CHUNK), :] = pltpu.roll(rows, turn, 1)[:, :256]
        return carry

    lax.fori_loop(0, 4, plane, 0)


def cut_inner(source, base, positions, out_x, out_y):
    depth_at, tile_at, _ = place()
    parity = lax.rem(depth_at, 2)
    for slot, out in ((1 - parity, out_x), (parity, out_y)):
        offset, col = window_offset(positions, slot, tile_at)
        cut(source, base + offset - 128 * slot, col, out)


def inner_kernel(positions, strip, out_x, out_y):
    cut_inner(strip, 0, positions, out_x, out_y)


VMEM = pl.BlockSpec(memory_space=pltpu.VMEM)


def run_inner(positions, strip):
    return pl.pallas_call(
        inner_kernel, out_shape=[HALF] * 2, in_specs=[SMEM, VMEM], out_specs=[VMEM] * 2, name="cut_inner"
    )(positions, strip)


def halo_kernel(positions, strip, above, below, out_x, out_y, canvas, sems):
    depth_at, tile_at, _ = place()
    copies = [
        pltpu.make_async_copy(above, canvas.at[0, :, :, pl.ds(0, 128), :], sems.at[0]),
        pltpu.make_async_copy(strip.at[:, :, pl.ds(0, 128), :], canvas.at[0, :, :, pl.ds(128, 128), :], sems.at[1]),
        pltpu.make_async_copy(strip.at[:, :, pl.ds(128, 128), :], canvas.at[1, :, :, pl.ds(0, 128), :], sems.at[2]),
        pltpu.make_async_copy(below, canvas.at[1, :, :, pl.ds(128, 128), :], sems.at[3]),
    ]
    for copy in copies:
        copy.start()
    for copy in copies:
        copy.wait()
    parity = lax.rem(depth_at, 2)
    for slot, out in ((1 - parity, out_x), (parity, out_y)):
        offset, col = window_offset(positions, slot, tile_at)
        cut(canvas.at[slot], offset - 128 * slot, col, out)


def run_halo(positions, strip, above, below):
    return pl.pallas_call(
        halo_kernel,
        out_shape=[HALF] * 2,
        in_specs=[SMEM] + [ANY] * 3,
        out_specs=[VMEM] * 2,
        scratch_shapes=[pltpu.VMEM((2, 2, 2, 256, 512), F32), pltpu.SemaphoreType.DMA((4,))],
        name="cut_halo",
    )(positions, strip, above, below)


def choose(options, pick, target, sem, wait):
    for number, option in enumerate(options):

        @pl.when(pick == number)
        def _(option=option):
            copy = pltpu.make_async_copy(option, target, sem)
            copy.wait() if wait else copy.start()


def by_slot(own, a, b, c):
    return ((own, a, c, b), (a, own, b, c))


def pick_kernel(own, a, b, c, up, down, sems):
    rel = place()[2]
    for wait in (False, True):
        for slot, target in ((0, up), (1, down)):
            choose(by_slot(own, a, b, c)[slot], rel, target, sems.at[slot], wait)


def run_pick(arrays):
    return pl.pallas_call(
        pick_kernel,
        out_shape=[HALF] * 2,
        in_specs=[ANY] * 4,
        out_specs=[ANY] * 2,
        scratch_shapes=[pltpu.SemaphoreType.DMA((2,))],
        name="pick_halo",
    )(*arrays)


def update_kernel(with_cut, positions, pos_above, pos_below, strip, *rest):
    inner, halo, (up, down) = rest[:4], rest[4:8], rest[8:10]
    outs, (canvas, grads, sems) = rest[10 : (13 if with_cut else 11)], rest[-3:]
    _, tile_at, rel = place()
    body = canvas.at[:, :, pl.ds(128, 256), :]
    load = pltpu.make_async_copy(strip, body, sems.at[6])
    fixed = [pltpu.make_async_copy(up, grads.at[4], sems.at[4]), pltpu.make_async_copy(down, grads.at[5], sems.at[5])]
    load.start()
    for wait in (False, True):
        for slot in range(2):
            choose(by_slot(*inner)[slot], rel, grads.at[slot], sems.at[slot], wait)
            choose(by_slot(*halo)[slot], rel, grads.at[2 + slot], sems.at[2 + slot], wait)
        for copy in fixed:
            copy.wait() if wait else copy.start()
    load.wait()
    off_0, col_0 = window_offset(positions, 0, tile_at)
    off_1, col_1 = window_offset(positions, 1, tile_at)
    off_up, col_up = window_offset(pos_above, 1, tile_at - 1)
    off_down, col_down = window_offset(pos_below, 0, tile_at + 1)
    up_row = jnp.clip(off_up - 128, 0, 128)
    down_row = jnp.clip(off_down, 0, 128) + 256
    spots = [
        (off_0 + 128, col_0),
        (off_1, col_1),
        (off_0, col_0),
        (off_1 + 128, col_1),
        (up_row, jnp.clip(col_up, 0, 256)),
        (down_row, jnp.clip(col_down, 0, 256)),
    ]

    def plane(number, carry):
        part, layer = number // 2, lax.rem(number, 2)
        for index, (row, col) in enumerate(spots):
            start = aligned(row, 512)
            for at in range(0, 128, CHUNK):
                value = grads[index, part, layer, pl.ds(at, CHUNK), :] * (-step_rate)
                wide = jnp.concatenate([value, jnp.zeros((8, 256), F32)], axis=0)
                wide = pltpu.roll(wide, row - start, 0)
                wide = jnp.concatenate([wide, jnp.zeros_like(wide)], axis=1)
                spot = (part, layer, pl.ds(start + at, CHUNK + 8), slice(None))
                canvas[spot] = canvas[spot] + pltpu.roll(wide, col, 1)
        return carry

    lax.fori_loop(0, 4, plane, 0)
    store = pltpu.make_async_copy(body, outs[0], sems.at[6])
    store.start()
    if with_cut:
        cut_inner(canvas, 128, positions, outs[1], outs[2])
    store.wait()


def run_update(with_cut, positions, pos_above, pos_below, strip, inner, halo, up, down):
    return pl.pallas_call(
        functools.partial(update_kernel, with_cut),
        out_shape=[jax.ShapeDtypeStruct((2, 2, 256, 512), F32)] + [HALF] * (2 * with_cut),
        in_specs=[SMEM] * 3 + [ANY] * 11,
        out_specs=[ANY] + [VMEM] * (2 * with_cut),
        scratch_shapes=[
            pltpu.VMEM((2, 2, 512, 512), F32),
            pltpu.VMEM((6, 2, 2, 128, 256), F32),
            pltpu.SemaphoreType.DMA((7,)),
        ],
        name=f"update_{int(with_cut)}",
    )(positions, pos_above, pos_below, strip, *inner, *halo, up, down)


def pairs(even, odd, tiles):
    return [
        (source * tiles + tile, target * tiles + tile)
        for tile in range(tiles)
        for source, target in (odd if tile % 2 else even)
    ]


def shards(transmission, probe, intensity, positions, batch):
    tiles = lax.axis_size("tile")
    depths = lax.axis_size("depth")
    table = jnp.asarray(operator_table(256))
    flows = [
        pairs([(1, 0), (0, 1)], [(3, 2), (2, 3)], tiles),
        pairs([(3, 0), (2, 1)], [(1, 2), (0, 3)], tiles),
        pairs([(2, 0), (3, 1)], [(0, 2), (1, 3)], tiles),
    ]
    returns = [[(b, a) for a, b in flow] for flow in flows]
    to_next = [(d * tiles + t, d * tiles + t + 1) for d in range(depths) for t in range(tiles - 1)]
    to_last = [(b, a) for a, b in to_next]

    def send(value, flow):
        return lax.ppermute(value, AXES, flow)

    strip = transmission
    pos_above = send(positions, to_next)
    pos_below = send(positions, to_last)
    x_inner, y_inner = run_inner(positions, strip)
    for turn_at in range(2):
        above = send(strip[:, :, 128:], to_next)
        below = send(strip[:, :, :128], to_last)
        inner = [y_inner] + [send(v, flow) for v, flow in zip((x_inner, x_inner, y_inner), flows)]
        x_halo, y_halo = run_halo(positions, strip, above, below)
        halo = [y_halo] + [send(v, flow) for v, flow in zip((x_halo, x_halo, y_halo), flows)]
        grads = run_main(turn_at, batch, probe, intensity, table, inner + halo)
        halo = [grads[4]] + [send(v, flow) for v, flow in zip(grads[5:], returns)]
        inner = [grads[0]] + [send(v, flow) for v, flow in zip(grads[1:4], returns)]
        to_up, to_down = run_pick(halo)
        from_below = send(to_up, to_last)
        from_above = send(to_down, to_next)
        result = run_update(turn_at == 0, positions, pos_above, pos_below, strip, inner, halo, from_above, from_below)
        strip = result[0]
        if turn_at == 0:
            x_inner, y_inner = result[1:]
    return strip


def solution(mesh):
    return jax.shard_map(
        shards,
        mesh=mesh,
        in_specs=(
            P(None, "depth", "tile", None),
            P(),
            P("tile", None, None),
            P("tile", None),
            P("tile"),
        ),
        out_specs=P(None, "depth", "tile", None),
        check_vma=False,
    )
```

```python
import functools
import math

import jax
import jax.numpy as jnp
import numpy as np
from jax import lax
from jax.experimental import pallas as pl
from jax.experimental.pallas import tpu as pltpu
from jax.sharding import PartitionSpec as P

prop_strength = 24.0
step_rate = 0.08

AXES = ("depth", "tile")
F32 = jnp.float32
BF16 = jnp.bfloat16
CHUNK = 32
STEP = 64


def operator_table(extent):
    counter = np.arange(extent)
    angles = 2.0 * np.pi / extent * (counter[:, None] * counter[None, :] % extent)
    far = (np.cos(angles) - 1j * np.sin(angles)) / math.sqrt(extent)
    freq = np.where(counter < extent // 2, counter, counter - extent) / extent
    turned = np.exp(-1j * np.pi * prop_strength * freq * freq)
    near = np.conj(far) @ (turned[:, None] * far)
    half = extent // 2
    blocks = [0.5 * (near[:half, :half] + sign * near[:half, half:]) for sign in (1, -1)]
    right = [np.block([[m.real, m.imag], [-m.imag, m.real]]) for m in blocks]
    parts = []
    for value in (*right, far.real, far.imag, far.real + far.imag):
        high = value.astype(BF16)
        low = (value - high.astype(np.float64)).astype(BF16)
        parts += [high, low]
    return np.stack(parts)


def place():
    depth_at = lax.axis_index("depth")
    tile_at = lax.axis_index("tile")
    rel = lax.rem(depth_at + 2 * lax.rem(tile_at, 2), 4)
    return depth_at, tile_at, rel


def split(x):
    high = x.astype(BF16)
    return high, (x - high.astype(F32)).astype(BF16)


def mm(a, b):
    return jnp.dot(a, b, preferred_element_type=F32)


def right_three(x, table, at):
    high, low = split(x)
    lhs = jnp.concatenate([high, high, low], axis=1)
    return mm(lhs, jnp.concatenate([table[at], table[at + 1], table[at]], axis=0))


def crossed(matrix):
    cat = jnp.concatenate
    upper = cat([matrix[:128, :128], matrix[128:, :128]], axis=1)
    return cat([upper, cat([matrix[:128, 128:], matrix[128:, 128:]], axis=1)], axis=0)


def left_three(x, table, at, view=lambda matrix: matrix):
    high, low = split(x)
    upper, lower = view(table[at]), view(table[at + 1])
    lhs = jnp.concatenate([upper, lower, upper], axis=1)
    return mm(lhs, jnp.concatenate([high, high, low], axis=0))


def far_two_sided(x_real, x_imag, table):
    for three in (right_three, left_three):
        first = three(x_real, table, 4)
        second = three(x_imag, table, 6)
        third = three(x_real + x_imag, table, 8)
        x_real, x_imag = first - second, third - first - second
    return x_real, x_imag


def near_two_sided(x_real, x_imag, table):
    cat = jnp.concatenate
    x_a = cat([x_real[:, :128], x_imag[:, :128]], axis=1)
    x_b = cat([x_real[:, 128:], x_imag[:, 128:]], axis=1)
    even, odd = right_three(x_a + x_b, table, 0), right_three(x_a - x_b, table, 2)
    u_a, u_b = even + odd, even - odd
    v_real = cat([u_a[:, :128], u_b[:, :128]], axis=1)
    v_imag = cat([u_a[:, 128:], u_b[:, 128:]], axis=1)
    v_a = cat([v_real[:128], v_imag[:128]], axis=0)
    v_b = cat([v_real[128:], v_imag[128:]], axis=0)
    even, odd = left_three(v_a + v_b, table, 0, crossed), left_three(v_a - v_b, table, 2, crossed)
    y_a, y_b = even + odd, even - odd
    return cat([y_a[:128], y_b[:128]], axis=0), cat([y_a[128:], y_b[128:]], axis=0)


def main_kernel(in_turn, probe, intensity, table_in, *rest):
    ins, outs, (obj, seen, wave, measured, table, sems) = rest[:8], rest[8:16], rest[16:]
    depth = 4
    depth_at, tile_at, rel = place()
    slot = lax.rem(rel, 2)
    is_dest = rel < 2
    active = is_dest & (in_turn[slot] > 0)
    near = 1 + 2 * slot
    chunks = [depth_at, lax.rem(depth_at + near, 4), lax.rem(depth_at + 4 - near, 4), lax.rem(depth_at + 2, 4)]
    row_inner = pl.multiple_of(128 * (1 - slot), 128)
    row_halo = pl.multiple_of(128 * slot, 128)

    def half(buffer, number):
        row = row_inner if number < 4 else row_halo
        return buffer.at[chunks[number % 4], :, :, pl.ds(row, 128), :]

    def store(n):
        return pltpu.make_async_copy(half(seen, n), outs[n], sems.at[1, n])

    def store_all():
        for n in range(8):
            store(n).start()

    @pl.when(active)
    def _():
        first = pltpu.make_async_copy(probe, wave, sems.at[2, 0])
        tables = pltpu.make_async_copy(table_in, table, sems.at[2, 1])
        level = pltpu.make_async_copy(intensity.at[slot], measured, sems.at[2, 2])
        first.start()
        tables.start()
        for n in range(8):
            pltpu.make_async_copy(ins[n], half(obj, n), sems.at[0, 2 * chunks[n % 4] + n // 4]).start()
        level.start()
        first.wait()
        tables.wait()

        def forward(at, carry):
            for n in range(2):
                pltpu.make_async_copy(ins[4 * n], half(obj, 4 * n), sems.at[0, 2 * at + n]).wait()
            for s in range(2):
                w_real, w_imag = wave[0], wave[1]
                seen[at, 0, s] = w_real
                seen[at, 1, s] = w_imag
                o_real, o_imag = obj[at, 0, s], obj[at, 1, s]
                wave[0], wave[1] = near_two_sided(
                    o_real * w_real - o_imag * w_imag, o_real * w_imag + o_imag * w_real, table
                )
            return carry

        lax.fori_loop(0, depth, forward, 0)
        level.wait()
        f_real, f_imag = far_two_sided(wave[0], wave[1], table)
        factor = 4.0 * (f_real * f_real + f_imag * f_imag - measured[...])
        wave[0], wave[1] = far_two_sided(factor * f_real, -(factor * f_imag), table)

        def backward(step, carry):
            at = depth - 1 - step
            for s in (1, 0):
                c_real, c_imag = near_two_sided(wave[0], wave[1], table)
                s_real, s_imag = seen[at, 0, s], seen[at, 1, s]
                seen[at, 0, s] = c_real * s_real - c_imag * s_imag
                seen[at, 1, s] = -(c_imag * s_real + c_real * s_imag)
                o_real, o_imag = obj[at, 0, s], obj[at, 1, s]
                wave[0] = o_real * c_real - o_imag * c_imag
                wave[1] = o_real * c_imag + o_imag * c_real
            for n in range(4):

                @pl.when(chunks[n] == at)
                def _(n=n):
                    store(n).start()
                    store(n + 4).start()

            return carry

        lax.fori_loop(0, depth, backward, 0)

    @pl.when(is_dest & jnp.logical_not(active))
    def _():
        seen[...] = jnp.zeros(seen.shape, F32)
        store_all()

    @pl.when(is_dest)
    def _():
        for n in range(8):
            store(n).wait()


ANY = pl.BlockSpec(memory_space=pl.ANY)
SMEM = pl.BlockSpec(memory_space=pltpu.SMEM)
HALF = jax.ShapeDtypeStruct((2, 2, 128, 256), F32)


def run_main(in_turn, probe, intensity, table, ins):
    return pl.pallas_call(
        main_kernel,
        out_shape=[HALF] * 8,
        in_specs=[SMEM] + [ANY] * 11,
        out_specs=[ANY] * 8,
        scratch_shapes=[
            pltpu.VMEM((4, 2, 2, 256, 256), F32),
            pltpu.VMEM((4, 2, 2, 256, 256), F32),
            pltpu.VMEM((2, 256, 256), F32),
            pltpu.VMEM((256, 256), F32),
            pltpu.VMEM((10, 256, 256), BF16),
            pltpu.SemaphoreType.DMA((3, 8)),
        ],
        compiler_params=pltpu.CompilerParams(vmem_limit_bytes=24 << 20),
        name="probe_chain",
    )(in_turn, probe, intensity, table, *ins)


VMEM = pl.BlockSpec(memory_space=pltpu.VMEM)
PLANES = 4


def window_offset(positions, slot, tile_at):
    return positions[slot, 0] - 256 * tile_at + 128, positions[slot, 1]


def aligned(row, extent, count):
    return pl.multiple_of(jnp.minimum(row // 8 * 8, extent - count - 8), 8)


def cut_columns(source, first, col, target, count):
    turn = lax.rem(512 - col, 512)
    for at in range(0, count, CHUNK):
        rows = source[pl.ds(first + at, CHUNK), :]
        target[pl.ds(at, CHUNK), :] = pltpu.roll(rows, turn, 1)[:, :256]


def cut_rows(source, first, target):
    start = aligned(first, 256, 128)
    shift = lax.rem(CHUNK + 8 - (first - start), CHUNK + 8)
    for at in range(0, 128, CHUNK):
        target[pl.ds(at, CHUNK), :] = pltpu.roll(source[pl.ds(start + at, CHUNK + 8), :], shift, 0)[:CHUNK]


def cut_all(source, base, positions, pos_above, pos_below, outs, columns):
    out_x, out_y, out_top, out_bottom, out_up, out_down = outs
    depth_at, tile_at, _ = place()
    parity = lax.rem(depth_at, 2)
    col_up = jnp.clip(pos_above[1, 1], 0, 256)
    col_down = jnp.clip(pos_below[0, 1], 0, 256)

    def plane(number, carry):
        part, layer = number // 2, lax.rem(number, 2)
        rows = source.at[part, layer]
        for slot in range(2):
            cut_columns(rows, base, positions[slot, 1], columns.at[slot], 256)
        cut_columns(rows, base, col_up, out_up.at[part, layer], 128)
        cut_columns(rows, base + 128, col_down, out_down.at[part, layer], 128)
        out_top[part, layer] = columns[0, :128]
        out_bottom[part, layer] = columns[1, 128:]
        for slot, out in ((1 - parity, out_x), (parity, out_y)):
            offset = window_offset(positions, slot, tile_at)[0]
            cut_rows(columns.at[slot], offset - 128 * slot, out.at[part, layer])
        return carry

    lax.fori_loop(0, PLANES, plane, 0)


def first_cut_kernel(positions, pos_above, pos_below, strip, *rest):
    cut_all(strip, 0, positions, pos_above, pos_below, rest[:6], rest[6])


COLUMNS = pltpu.VMEM((2, 256, 256), F32)


def run_first_cut(positions, pos_above, pos_below, strip):
    return pl.pallas_call(
        first_cut_kernel,
        out_shape=[HALF] * 6,
        in_specs=[SMEM] * 3 + [VMEM],
        out_specs=[VMEM] * 6,
        scratch_shapes=[COLUMNS],
        compiler_params=pltpu.CompilerParams(vmem_limit_bytes=16 << 20),
        name="first_cut",
    )(positions, pos_above, pos_below, strip)


def halo_kernel(positions, top, bottom, above, below, out_x, out_y, canvas, sems):
    depth_at, tile_at, _ = place()
    copies = [
        pltpu.make_async_copy(source, canvas.at[slot, :, :, pl.ds(row, 128), :], sems.at[number])
        for number, (source, slot, row) in enumerate(((above, 0, 0), (top, 0, 128), (bottom, 1, 0), (below, 1, 128)))
    ]
    for copy in copies:
        copy.start()
    for copy in copies:
        copy.wait()
    parity = lax.rem(depth_at, 2)

    def plane(number, carry):
        part, layer = number // 2, lax.rem(number, 2)
        for slot, out in ((1 - parity, out_x), (parity, out_y)):
            offset = window_offset(positions, slot, tile_at)[0]
            cut_rows(canvas.at[slot, part, layer], offset - 128 * slot, out.at[part, layer])
        return carry

    lax.fori_loop(0, PLANES, plane, 0)


def run_halo(positions, top, bottom, above, below):
    return pl.pallas_call(
        halo_kernel,
        out_shape=[HALF] * 2,
        in_specs=[SMEM] + [ANY] * 4,
        out_specs=[VMEM] * 2,
        scratch_shapes=[pltpu.VMEM((2, 2, 2, 256, 256), F32), pltpu.SemaphoreType.DMA((4,))],
        compiler_params=pltpu.CompilerParams(vmem_limit_bytes=12 << 20),
        name="cut_halo",
    )(positions, top, bottom, above, below)


def by_slot(own, a, b, c, rel):
    first = jnp.where(rel == 0, own, jnp.where(rel == 1, a, jnp.where(rel == 2, c, b)))
    second = jnp.where(rel == 0, a, jnp.where(rel == 1, own, jnp.where(rel == 2, b, c)))
    return first, second


def update_kernel(with_cut, positions, pos_above, pos_below, strip, *rest):
    ins, outs, (canvas, windows, edges, columns, sems) = rest[:6], rest[6:-5], rest[-5:]
    tile_at = place()[1]
    body = canvas.at[:, :, pl.ds(128, 256), :]
    spots = [(windows.at[0], 128), (windows.at[1], 0), (windows.at[0], 0), (windows.at[1], 128)]
    targets = [to.at[:, :, pl.ds(row, 128), :] for to, row in spots] + [edges.at[0], edges.at[1]]
    copies = [pltpu.make_async_copy(strip, body, sems.at[6])]
    copies += [pltpu.make_async_copy(ins[n], targets[n], sems.at[n]) for n in range(6)]
    for copy in copies:
        copy.start()
    for copy in copies:
        copy.wait()
    off_0, col_0 = window_offset(positions, 0, tile_at)
    off_1, col_1 = window_offset(positions, 1, tile_at)
    off_up, col_up = window_offset(pos_above, 1, tile_at - 1)
    off_down, col_down = window_offset(pos_below, 0, tile_at + 1)
    pieces = [
        (windows.at[0], 256, off_0, col_0),
        (windows.at[1], 256, off_1, col_1),
        (edges.at[0], 128, jnp.clip(off_up - 128, 0, 128), jnp.clip(col_up, 0, 256)),
        (edges.at[1], 128, jnp.clip(off_down, 0, 128) + 256, jnp.clip(col_down, 0, 256)),
    ]

    def plane(number, carry):
        part, layer = number // 2, lax.rem(number, 2)
        for source, count, row, col in pieces:
            start = aligned(row, 512, count)
            for at in range(0, count, STEP):
                value = source[part, layer, pl.ds(at, STEP), :] * (-step_rate)
                wide = jnp.concatenate([value, jnp.zeros((8, 256), F32)], axis=0)
                wide = pltpu.roll(wide, row - start, 0)
                wide = jnp.concatenate([wide, jnp.zeros_like(wide)], axis=1)
                spot = (part, layer, pl.ds(start + at, STEP + 8), slice(None))
                canvas[spot] = canvas[spot] + pltpu.roll(wide, col, 1)
        return carry

    lax.fori_loop(0, PLANES, plane, 0)
    store = pltpu.make_async_copy(body, outs[0], sems.at[6])
    store.start()
    if with_cut:
        cut_all(canvas, 128, positions, pos_above, pos_below, outs[1:], columns)
    store.wait()


def run_update(with_cut, positions, pos_above, pos_below, strip, parts):
    return pl.pallas_call(
        functools.partial(update_kernel, with_cut),
        out_shape=[jax.ShapeDtypeStruct((2, 2, 256, 512), F32)] + [HALF] * (6 * with_cut),
        in_specs=[SMEM] * 3 + [ANY] * 7,
        out_specs=[ANY] + [VMEM] * (6 * with_cut),
        scratch_shapes=[
            pltpu.VMEM((2, 2, 512, 512), F32),
            pltpu.VMEM((2, 2, 2, 256, 256), F32),
            pltpu.VMEM((2, 2, 2, 128, 256), F32),
            COLUMNS,
            pltpu.SemaphoreType.DMA((7,)),
        ],
        compiler_params=pltpu.CompilerParams(vmem_limit_bytes=20 << 20),
        name=f"update_{int(with_cut)}",
    )(positions, pos_above, pos_below, strip, *parts)


def pairs(even, odd, tiles):
    return [
        (source * tiles + tile, target * tiles + tile)
        for tile in range(tiles)
        for source, target in (odd if tile % 2 else even)
    ]


def shards(transmission, probe, intensity, positions, batch):
    tiles = lax.axis_size("tile")
    depths = lax.axis_size("depth")
    table = jnp.asarray(operator_table(256))
    flows = [
        pairs([(1, 0), (0, 1)], [(3, 2), (2, 3)], tiles),
        pairs([(3, 0), (2, 1)], [(1, 2), (0, 3)], tiles),
        pairs([(2, 0), (3, 1)], [(0, 2), (1, 3)], tiles),
    ]
    returns = [[(b, a) for a, b in flow] for flow in flows]
    to_next = [(d * tiles + t, d * tiles + t + 1) for d in range(depths) for t in range(tiles - 1)]
    to_last = [(b, a) for a, b in to_next]

    def send(value, flow):
        return lax.ppermute(value, AXES, flow)

    rel = place()[2]
    strip = transmission
    pos_above = send(positions, to_next)
    pos_below = send(positions, to_last)
    cuts = run_first_cut(positions, pos_above, pos_below, strip)
    for turn_at in range(2):
        x_inner, y_inner, top, bottom, up, down = cuts
        above = send(down, to_next)
        below = send(up, to_last)
        inner = [y_inner] + [send(v, flow) for v, flow in zip((x_inner, x_inner, y_inner), flows)]
        x_halo, y_halo = run_halo(positions, top, bottom, above, below)
        halo = [y_halo] + [send(v, flow) for v, flow in zip((x_halo, x_halo, y_halo), flows)]
        grads = run_main((batch == turn_at).astype(jnp.int32), probe, intensity, table, inner + halo)
        halo = [grads[4]] + [send(v, flow) for v, flow in zip(grads[5:], returns)]
        inner = [grads[0]] + [send(v, flow) for v, flow in zip(grads[1:4], returns)]
        to_up, to_down = by_slot(*halo, rel)
        from_below = send(to_up, to_last)
        from_above = send(to_down, to_next)
        parts = [*by_slot(*inner, rel), to_up, to_down, from_above, from_below]
        result = run_update(turn_at == 0, positions, pos_above, pos_below, strip, parts)
        strip, cuts = result[0], result[1:]
    return strip


def solution(mesh):
    return jax.shard_map(
        shards,
        mesh=mesh,
        in_specs=(
            P(None, "depth", "tile", None),
            P(),
            P("tile", None, None),
            P("tile", None),
            P("tile"),
        ),
        out_specs=P(None, "depth", "tile", None),
        check_vma=False,
    )
```

```python
import functools
import math

import jax
import jax.numpy as jnp
import numpy as np
from jax import lax
from jax.experimental import pallas as pl
from jax.experimental.pallas import tpu as pltpu
from jax.sharding import PartitionSpec as P

prop_strength = 24.0
step_rate = 0.08

AXES = ("depth", "tile")
F32 = jnp.float32
BF16 = jnp.bfloat16
CHUNK = 32
STEP = 64


def operator_table(extent):
    counter = np.arange(extent)
    angles = 2.0 * np.pi / extent * (counter[:, None] * counter[None, :] % extent)
    far = (np.cos(angles) - 1j * np.sin(angles)) / math.sqrt(extent)
    freq = np.where(counter < extent // 2, counter, counter - extent) / extent
    turned = np.exp(-1j * np.pi * prop_strength * freq * freq)
    near = np.conj(far) @ (turned[:, None] * far)
    half = extent // 2
    blocks = [0.5 * (near[:half, :half] + sign * near[:half, half:]) for sign in (1, -1)]
    right = [np.block([[m.real, m.imag], [-m.imag, m.real]]) for m in blocks]
    parts = []
    for value in (*right, far.real, far.imag, far.real + far.imag):
        high = value.astype(BF16)
        low = (value - high.astype(np.float64)).astype(BF16)
        parts += [high, low]
    return np.stack(parts)


def place():
    depth_at = lax.axis_index("depth")
    tile_at = lax.axis_index("tile")
    rel = lax.rem(depth_at + 2 * lax.rem(tile_at, 2), 4)
    return depth_at, tile_at, rel


def split(x):
    high = x.astype(BF16)
    return high, (x - high.astype(F32)).astype(BF16)


def mm(a, b):
    return jnp.dot(a, b, preferred_element_type=F32)


def right_three(x, table, at):
    high, low = split(x)
    lhs = jnp.concatenate([high, high, low], axis=1)
    return mm(lhs, jnp.concatenate([table[at], table[at + 1], table[at]], axis=0))


def crossed(matrix):
    cat = jnp.concatenate
    upper = cat([matrix[:128, :128], matrix[128:, :128]], axis=1)
    return cat([upper, cat([matrix[:128, 128:], matrix[128:, 128:]], axis=1)], axis=0)


def left_three(x, table, at, view=lambda matrix: matrix):
    high, low = split(x)
    upper, lower = view(table[at]), view(table[at + 1])
    lhs = jnp.concatenate([upper, lower, upper], axis=1)
    return mm(lhs, jnp.concatenate([high, high, low], axis=0))


def far_two_sided(x_real, x_imag, table):
    for three in (right_three, left_three):
        first = three(x_real, table, 4)
        second = three(x_imag, table, 6)
        third = three(x_real + x_imag, table, 8)
        x_real, x_imag = first - second, third - first - second
    return x_real, x_imag


def near_two_sided(x_real, x_imag, table):
    cat = jnp.concatenate
    x_a = cat([x_real[:, :128], x_imag[:, :128]], axis=1)
    x_b = cat([x_real[:, 128:], x_imag[:, 128:]], axis=1)
    even, odd = right_three(x_a + x_b, table, 0), right_three(x_a - x_b, table, 2)
    u_a, u_b = even + odd, even - odd
    v_real = cat([u_a[:, :128], u_b[:, :128]], axis=1)
    v_imag = cat([u_a[:, 128:], u_b[:, 128:]], axis=1)
    v_a = cat([v_real[:128], v_imag[:128]], axis=0)
    v_b = cat([v_real[128:], v_imag[128:]], axis=0)
    even, odd = left_three(v_a + v_b, table, 0, crossed), left_three(v_a - v_b, table, 2, crossed)
    y_a, y_b = even + odd, even - odd
    return cat([y_a[:128], y_b[:128]], axis=0), cat([y_a[128:], y_b[128:]], axis=0)


def main_kernel(in_turn, _, __, probe, intensity, table_in, *rest):
    ins, outs, (obj, seen, wave, measured, table, sems) = rest[:8], rest[8:16], rest[16:]
    depth = 4
    depth_at, tile_at, rel = place()
    slot = lax.rem(rel, 2)
    is_dest = rel < 2
    active = is_dest & (in_turn[slot] > 0)
    near = 1 + 2 * slot
    chunks = [depth_at, lax.rem(depth_at + near, 4), lax.rem(depth_at + 4 - near, 4), lax.rem(depth_at + 2, 4)]
    row_inner = pl.multiple_of(128 * (1 - slot), 128)
    row_halo = pl.multiple_of(128 * slot, 128)

    def half(buffer, number):
        row = row_inner if number < 4 else row_halo
        return buffer.at[chunks[number % 4], :, :, pl.ds(row, 128), :]

    def store(n):
        return pltpu.make_async_copy(half(seen, n), outs[n], sems.at[1, n])

    def store_all():
        for n in range(8):
            store(n).start()

    @pl.when(active)
    def _():
        first = pltpu.make_async_copy(probe, wave, sems.at[2, 0])
        tables = pltpu.make_async_copy(table_in, table, sems.at[2, 1])
        level = pltpu.make_async_copy(intensity.at[slot], measured, sems.at[2, 2])
        first.start()
        tables.start()
        for n in range(8):
            pltpu.make_async_copy(ins[n], half(obj, n), sems.at[0, 2 * chunks[n % 4] + n // 4]).start()
        level.start()
        first.wait()
        tables.wait()

        def forward(at, carry):
            for n in range(2):
                pltpu.make_async_copy(ins[4 * n], half(obj, 4 * n), sems.at[0, 2 * at + n]).wait()
            for s in range(2):
                w_real, w_imag = wave[0], wave[1]
                seen[at, 0, s] = w_real
                seen[at, 1, s] = w_imag
                o_real, o_imag = obj[at, 0, s], obj[at, 1, s]
                wave[0], wave[1] = near_two_sided(
                    o_real * w_real - o_imag * w_imag, o_real * w_imag + o_imag * w_real, table
                )
            return carry

        lax.fori_loop(0, depth, forward, 0)
        level.wait()
        f_real, f_imag = far_two_sided(wave[0], wave[1], table)
        factor = 4.0 * (f_real * f_real + f_imag * f_imag - measured[...])
        wave[0], wave[1] = far_two_sided(factor * f_real, -(factor * f_imag), table)

        def backward(step, carry):
            at = depth - 1 - step
            for s in (1, 0):
                c_real, c_imag = near_two_sided(wave[0], wave[1], table)
                s_real, s_imag = seen[at, 0, s], seen[at, 1, s]
                seen[at, 0, s] = c_real * s_real - c_imag * s_imag
                seen[at, 1, s] = -(c_imag * s_real + c_real * s_imag)
                o_real, o_imag = obj[at, 0, s], obj[at, 1, s]
                wave[0] = o_real * c_real - o_imag * c_imag
                wave[1] = o_real * c_imag + o_imag * c_real
            for n in range(4):

                @pl.when(chunks[n] == at)
                def _(n=n):
                    store(n).start()
                    store(n + 4).start()

            return carry

        lax.fori_loop(0, depth, backward, 0)

    @pl.when(is_dest & jnp.logical_not(active))
    def _():
        seen[...] = jnp.zeros(seen.shape, F32)
        store_all()

    @pl.when(is_dest)
    def _():
        for n in range(8):
            store(n).wait()


ANY = pl.BlockSpec(memory_space=pl.ANY)
SMEM = pl.BlockSpec(memory_space=pltpu.SMEM)
HALF = jax.ShapeDtypeStruct((2, 2, 128, 256), F32)


def run_main(in_turn, pos_above, pos_below, probe, intensity, table, ins):
    return pl.pallas_call(
        main_kernel,
        out_shape=[pltpu.HBM(HALF.shape, F32)] * 8,
        in_specs=[SMEM] * 3 + [ANY] * 11,
        out_specs=[pl.BlockSpec(memory_space=pltpu.HBM)] * 8,
        scratch_shapes=[
            pltpu.VMEM((4, 2, 2, 256, 256), F32),
            pltpu.VMEM((4, 2, 2, 256, 256), F32),
            pltpu.VMEM((2, 256, 256), F32),
            pltpu.VMEM((256, 256), F32),
            pltpu.VMEM((10, 256, 256), BF16),
            pltpu.SemaphoreType.DMA((3, 8)),
        ],
        compiler_params=pltpu.CompilerParams(vmem_limit_bytes=24 << 20),
        name="probe_chain",
    )(in_turn, pos_above, pos_below, probe, intensity, table, *ins)


VMEM = pl.BlockSpec(memory_space=pltpu.VMEM)
PLANES = 4


def window_offset(positions, slot, tile_at):
    return positions[slot, 0] - 256 * tile_at + 128, positions[slot, 1]


def aligned(row, extent, count):
    return pl.multiple_of(jnp.minimum(row // 8 * 8, extent - count - 8), 8)


def cut_columns(source, first, col, target, count):
    turn = lax.rem(512 - col, 512)
    for at in range(0, count, CHUNK):
        rows = source[pl.ds(first + at, CHUNK), :]
        target[pl.ds(at, CHUNK), :] = pltpu.roll(rows, turn, 1)[:, :256]


def cut_rows(source, first, target):
    start = aligned(first, 256, 128)
    shift = lax.rem(CHUNK + 8 - (first - start), CHUNK + 8)
    for at in range(0, 128, CHUNK):
        target[pl.ds(at, CHUNK), :] = pltpu.roll(source[pl.ds(start + at, CHUNK + 8), :], shift, 0)[:CHUNK]


def cut_all(source, base, positions, pos_above, pos_below, outs, columns):
    out_x, out_y, out_top, out_bottom, out_up, out_down = outs
    depth_at, tile_at, _ = place()
    parity = lax.rem(depth_at, 2)
    col_up = jnp.clip(pos_above[1, 1], 0, 256)
    col_down = jnp.clip(pos_below[0, 1], 0, 256)

    def plane(number, carry):
        part, layer = number // 2, lax.rem(number, 2)
        rows = source.at[part, layer]
        for slot in range(2):
            cut_columns(rows, base, positions[slot, 1], columns.at[slot], 256)
        cut_columns(rows, base, col_up, out_up.at[part, layer], 128)
        cut_columns(rows, base + 128, col_down, out_down.at[part, layer], 128)
        out_top[part, layer] = columns[0, :128]
        out_bottom[part, layer] = columns[1, 128:]
        for slot, out in ((1 - parity, out_x), (parity, out_y)):
            offset = window_offset(positions, slot, tile_at)[0]
            cut_rows(columns.at[slot], offset - 128 * slot, out.at[part, layer])
        return carry

    lax.fori_loop(0, PLANES, plane, 0)


def inner_kernel(positions, strip, out_x, out_y, columns):
    depth_at, tile_at, _ = place()
    parity = lax.rem(depth_at, 2)

    def plane(number, carry):
        part, layer = number // 2, lax.rem(number, 2)
        for slot, out in ((1 - parity, out_x), (parity, out_y)):
            offset, col = window_offset(positions, slot, tile_at)
            cut_columns(strip.at[part, layer], 0, col, columns.at[0], 256)
            cut_rows(columns.at[0], offset - 128 * slot, out.at[part, layer])
        return carry

    lax.fori_loop(0, PLANES, plane, 0)


COLUMNS = pltpu.VMEM((2, 256, 256), F32)


def run_inner(positions, strip):
    return pl.pallas_call(
        inner_kernel,
        out_shape=[HALF] * 2,
        in_specs=[SMEM, VMEM],
        out_specs=[VMEM] * 2,
        scratch_shapes=[COLUMNS],
        compiler_params=pltpu.CompilerParams(vmem_limit_bytes=12 << 20),
        name="cut_inner",
    )(positions, strip)


def wide_halo_kernel(positions, strip, above, below, out_x, out_y, columns):
    depth_at, tile_at, _ = place()
    parity = lax.rem(depth_at, 2)

    def plane(number, carry):
        part, layer = number // 2, lax.rem(number, 2)
        own = strip.at[part, layer]
        for slot, (source, row, own_row) in enumerate(((above, 0, 128), (below, 128, 0))):
            col = positions[slot, 1]
            cut_columns(source.at[part, layer], 0, col, columns.at[slot, pl.ds(row, 128), :], 128)
            cut_columns(own, 128 * slot, col, columns.at[slot, pl.ds(own_row, 128), :], 128)
        for slot, out in ((1 - parity, out_x), (parity, out_y)):
            offset = window_offset(positions, slot, tile_at)[0]
            cut_rows(columns.at[slot], offset - 128 * slot, out.at[part, layer])
        return carry

    lax.fori_loop(0, PLANES, plane, 0)


def run_wide_halo(positions, strip, above, below):
    return pl.pallas_call(
        wide_halo_kernel,
        out_shape=[HALF] * 2,
        in_specs=[SMEM] + [VMEM] * 3,
        out_specs=[VMEM] * 2,
        scratch_shapes=[COLUMNS],
        compiler_params=pltpu.CompilerParams(vmem_limit_bytes=12 << 20),
        name="cut_wide_halo",
    )(positions, strip, above, below)


def halo_kernel(positions, top, bottom, above, below, out_x, out_y, canvas, sems):
    depth_at, tile_at, _ = place()
    copies = [
        pltpu.make_async_copy(source, canvas.at[slot, :, :, pl.ds(row, 128), :], sems.at[number])
        for number, (source, slot, row) in enumerate(((above, 0, 0), (top, 0, 128), (bottom, 1, 0), (below, 1, 128)))
    ]
    for copy in copies:
        copy.start()
    for copy in copies:
        copy.wait()
    parity = lax.rem(depth_at, 2)

    def plane(number, carry):
        part, layer = number // 2, lax.rem(number, 2)
        for slot, out in ((1 - parity, out_x), (parity, out_y)):
            offset = window_offset(positions, slot, tile_at)[0]
            cut_rows(canvas.at[slot, part, layer], offset - 128 * slot, out.at[part, layer])
        return carry

    lax.fori_loop(0, PLANES, plane, 0)


def run_halo(positions, top, bottom, above, below):
    return pl.pallas_call(
        halo_kernel,
        out_shape=[HALF] * 2,
        in_specs=[SMEM] + [ANY] * 4,
        out_specs=[VMEM] * 2,
        scratch_shapes=[pltpu.VMEM((2, 2, 2, 256, 256), F32), pltpu.SemaphoreType.DMA((4,))],
        compiler_params=pltpu.CompilerParams(vmem_limit_bytes=12 << 20),
        name="cut_halo",
    )(positions, top, bottom, above, below)


def by_slot(own, a, b, c, rel):
    first = jnp.where(rel == 0, own, jnp.where(rel == 1, a, jnp.where(rel == 2, c, b)))
    second = jnp.where(rel == 0, a, jnp.where(rel == 1, own, jnp.where(rel == 2, b, c)))
    return first, second


def update_kernel(with_cut, positions, pos_above, pos_below, strip, *rest):
    ins, outs, (canvas, columns, sem) = rest[:6], rest[6:-3], rest[-3:]
    tile_at = place()[1]
    off_0, col_0 = window_offset(positions, 0, tile_at)
    off_1, col_1 = window_offset(positions, 1, tile_at)
    off_up, col_up = window_offset(pos_above, 1, tile_at - 1)
    off_down, col_down = window_offset(pos_below, 0, tile_at + 1)
    rows = (
        off_0 + 128,
        off_1,
        off_0,
        off_1 + 128,
        jnp.clip(off_up - 128, 0, 128),
        jnp.clip(off_down, 0, 128) + 256,
    )
    cols = (col_0, col_1, col_0, col_1, jnp.clip(col_up, 0, 256), jnp.clip(col_down, 0, 256))

    def plane(number, carry):
        part, layer = number // 2, lax.rem(number, 2)
        for at in range(0, 256, CHUNK):
            canvas[part, layer, pl.ds(128 + at, CHUNK), :] = strip[part, layer, pl.ds(at, CHUNK), :]
        for source, row, col in zip(ins, rows, cols):
            start = aligned(row, 512, 128)
            for at in range(0, 128, STEP):
                value = source[part, layer, pl.ds(at, STEP), :] * (-step_rate)
                wide = jnp.concatenate([value, jnp.zeros((8, 256), F32)], axis=0)
                wide = pltpu.roll(wide, row - start, 0)
                wide = jnp.concatenate([wide, jnp.zeros_like(wide)], axis=1)
                spot = (part, layer, pl.ds(start + at, STEP + 8), slice(None))
                canvas[spot] = canvas[spot] + pltpu.roll(wide, col, 1)
        return carry

    lax.fori_loop(0, PLANES, plane, 0)
    store = pltpu.make_async_copy(canvas.at[:, :, pl.ds(128, 256), :], outs[0], sem)
    store.start()
    if with_cut:
        cut_all(canvas, 128, positions, pos_above, pos_below, outs[1:], columns)
    store.wait()


def run_update(with_cut, positions, pos_above, pos_below, strip, parts):
    return pl.pallas_call(
        functools.partial(update_kernel, with_cut),
        out_shape=[jax.ShapeDtypeStruct((2, 2, 256, 512), F32)] + [HALF] * (6 * with_cut),
        in_specs=[SMEM] * 3 + [VMEM] * 7,
        out_specs=[ANY] + [VMEM] * (6 * with_cut),
        scratch_shapes=[pltpu.VMEM((2, 2, 512, 512), F32), COLUMNS, pltpu.SemaphoreType.DMA],
        compiler_params=pltpu.CompilerParams(vmem_limit_bytes=16 << 20),
        name=f"update_{int(with_cut)}",
    )(positions, pos_above, pos_below, strip, *parts)


def pairs(even, odd, tiles):
    return [
        (source * tiles + tile, target * tiles + tile)
        for tile in range(tiles)
        for source, target in (odd if tile % 2 else even)
    ]


def shards(transmission, probe, intensity, positions, batch):
    tiles = lax.axis_size("tile")
    depths = lax.axis_size("depth")
    table = jnp.asarray(operator_table(256))
    flows = [
        pairs([(1, 0), (0, 1)], [(3, 2), (2, 3)], tiles),
        pairs([(3, 0), (2, 1)], [(1, 2), (0, 3)], tiles),
        pairs([(2, 0), (3, 1)], [(0, 2), (1, 3)], tiles),
    ]
    returns = [[(b, a) for a, b in flow] for flow in flows]
    to_next = [(d * tiles + t, d * tiles + t + 1) for d in range(depths) for t in range(tiles - 1)]
    to_last = [(b, a) for a, b in to_next]

    def send(value, flow):
        return lax.ppermute(value, AXES, flow)

    rel = place()[2]
    strip = transmission
    pos_above = send(positions, to_next)
    pos_below = send(positions, to_last)
    for turn_at in range(2):
        if turn_at == 0:
            above = send(strip[:, :, 128:], to_next)
            below = send(strip[:, :, :128], to_last)
            x_inner, y_inner = run_inner(positions, strip)
        else:
            x_inner, y_inner, top, bottom, up, down = cuts
            above = send(down, to_next)
            below = send(up, to_last)
        inner = [y_inner] + [send(v, flow) for v, flow in zip((x_inner, x_inner, y_inner), flows)]
        if turn_at == 0:
            x_halo, y_halo = run_wide_halo(positions, strip, above, below)
        else:
            x_halo, y_halo = run_halo(positions, top, bottom, above, below)
        halo = [y_halo] + [send(v, flow) for v, flow in zip((x_halo, x_halo, y_halo), flows)]
        grads = run_main((batch == turn_at).astype(jnp.int32), pos_above, pos_below, probe, intensity, table, inner + halo)
        halo = [grads[4]] + [send(v, flow) for v, flow in zip(grads[5:], returns)]
        inner = [grads[0]] + [send(v, flow) for v, flow in zip(grads[1:4], returns)]
        to_up, to_down = by_slot(*halo, rel)
        from_below = send(to_up, to_last)
        from_above = send(to_down, to_next)
        parts = [*by_slot(*inner, rel), to_up, to_down, from_above, from_below]
        result = run_update(turn_at == 0, positions, pos_above, pos_below, strip, parts)
        strip, cuts = result[0], result[1:]
    return strip


def solution(mesh):
    return jax.shard_map(
        shards,
        mesh=mesh,
        in_specs=(
            P(None, "depth", "tile", None),
            P(),
            P("tile", None, None),
            P("tile", None),
            P("tile"),
        ),
        out_specs=P(None, "depth", "tile", None),
        check_vma=False,
    )
```

```python
import functools
import math

import jax
import jax.numpy as jnp
import numpy as np
from jax import lax
from jax.experimental import pallas as pl
from jax.experimental.pallas import tpu as pltpu
from jax.sharding import PartitionSpec as P

prop_strength = 24.0
step_rate = 0.08

AXES = ("depth", "tile")
F32 = jnp.float32
BF16 = jnp.bfloat16
CHUNK = 32
STEP = 64


def operator_table(extent):
    counter = np.arange(extent)
    angles = 2.0 * np.pi / extent * (counter[:, None] * counter[None, :] % extent)
    far = (np.cos(angles) - 1j * np.sin(angles)) / math.sqrt(extent)
    freq = np.where(counter < extent // 2, counter, counter - extent) / extent
    turned = np.exp(-1j * np.pi * prop_strength * freq * freq)
    near = np.conj(far) @ (turned[:, None] * far)
    half = extent // 2
    blocks = [0.5 * (near[:half, :half] + sign * near[:half, half:]) for sign in (1, -1)]
    right = [np.block([[m.real, m.imag], [-m.imag, m.real]]) for m in blocks]
    parts = []
    for value in (*right, far.real, far.imag, far.real + far.imag):
        high = value.astype(BF16)
        low = (value - high.astype(np.float64)).astype(BF16)
        parts += [high, low]
    return np.stack(parts)


def place():
    depth_at = lax.axis_index("depth")
    tile_at = lax.axis_index("tile")
    rel = lax.rem(depth_at + 2 * lax.rem(tile_at, 2), 4)
    return depth_at, tile_at, rel


def split(x):
    high = x.astype(BF16)
    return high, (x - high.astype(F32)).astype(BF16)


def mm(a, b):
    return jnp.dot(a, b, preferred_element_type=F32)


def right_three(x, table, at):
    high, low = split(x)
    lhs = jnp.concatenate([high, high, low], axis=1)
    return mm(lhs, jnp.concatenate([table[at], table[at + 1], table[at]], axis=0))


def crossed(matrix):
    cat = jnp.concatenate
    upper = cat([matrix[:128, :128], matrix[128:, :128]], axis=1)
    return cat([upper, cat([matrix[:128, 128:], matrix[128:, 128:]], axis=1)], axis=0)


def left_three(x, table, at, view=lambda matrix: matrix):
    high, low = split(x)
    upper, lower = view(table[at]), view(table[at + 1])
    lhs = jnp.concatenate([upper, lower, upper], axis=1)
    return mm(lhs, jnp.concatenate([high, high, low], axis=0))


def far_two_sided(x_real, x_imag, table):
    for three in (right_three, left_three):
        first = three(x_real, table, 4)
        second = three(x_imag, table, 6)
        third = three(x_real + x_imag, table, 8)
        x_real, x_imag = first - second, third - first - second
    return x_real, x_imag


def near_two_sided(x_real, x_imag, table):
    cat = jnp.concatenate
    x_a = cat([x_real[:, :128], x_imag[:, :128]], axis=1)
    x_b = cat([x_real[:, 128:], x_imag[:, 128:]], axis=1)
    even, odd = right_three(x_a + x_b, table, 0), right_three(x_a - x_b, table, 2)
    u_a, u_b = even + odd, even - odd
    v_real = cat([u_a[:, :128], u_b[:, :128]], axis=1)
    v_imag = cat([u_a[:, 128:], u_b[:, 128:]], axis=1)
    v_a = cat([v_real[:128], v_imag[:128]], axis=0)
    v_b = cat([v_real[128:], v_imag[128:]], axis=0)
    even, odd = left_three(v_a + v_b, table, 0, crossed), left_three(v_a - v_b, table, 2, crossed)
    y_a, y_b = even + odd, even - odd
    return cat([y_a[:128], y_b[:128]], axis=0), cat([y_a[128:], y_b[128:]], axis=0)


def main_kernel(in_turn, _, __, probe, intensity, table, *rest):
    ins, outs, (obj, seen, wave, sems) = rest[:8], rest[8:16], rest[16:]
    depth = 4
    depth_at, tile_at, rel = place()
    slot = lax.rem(rel, 2)
    is_dest = rel < 2
    active = is_dest & (in_turn[slot] > 0)
    near = 1 + 2 * slot
    chunks = [depth_at, lax.rem(depth_at + near, 4), lax.rem(depth_at + 4 - near, 4), lax.rem(depth_at + 2, 4)]
    row_inner = pl.multiple_of(128 * (1 - slot), 128)
    row_halo = pl.multiple_of(128 * slot, 128)

    def half(buffer, number):
        row = row_inner if number < 4 else row_halo
        return buffer.at[chunks[number % 4], :, :, pl.ds(row, 128), :]

    def store(n):
        return pltpu.make_async_copy(half(seen, n), outs[n], sems.at[1, n])

    def store_all():
        for n in range(8):
            store(n).start()

    @pl.when(active)
    def _():
        for n in range(8):
            pltpu.make_async_copy(ins[n], half(obj, n), sems.at[0, 2 * chunks[n % 4] + n // 4]).start()
        wave[...] = probe[...]

        def forward(at, carry):
            for n in range(2):
                pltpu.make_async_copy(ins[4 * n], half(obj, 4 * n), sems.at[0, 2 * at + n]).wait()
            for s in range(2):
                w_real, w_imag = wave[0], wave[1]
                seen[at, 0, s] = w_real
                seen[at, 1, s] = w_imag
                o_real, o_imag = obj[at, 0, s], obj[at, 1, s]
                wave[0], wave[1] = near_two_sided(
                    o_real * w_real - o_imag * w_imag, o_real * w_imag + o_imag * w_real, table
                )
            return carry

        lax.fori_loop(0, depth, forward, 0)
        f_real, f_imag = far_two_sided(wave[0], wave[1], table)
        factor = 4.0 * (f_real * f_real + f_imag * f_imag - intensity[slot])
        wave[0], wave[1] = far_two_sided(factor * f_real, -(factor * f_imag), table)

        def backward(step, carry):
            at = depth - 1 - step
            for s in (1, 0):
                c_real, c_imag = near_two_sided(wave[0], wave[1], table)
                s_real, s_imag = seen[at, 0, s], seen[at, 1, s]
                seen[at, 0, s] = c_real * s_real - c_imag * s_imag
                seen[at, 1, s] = -(c_imag * s_real + c_real * s_imag)
                o_real, o_imag = obj[at, 0, s], obj[at, 1, s]
                wave[0] = o_real * c_real - o_imag * c_imag
                wave[1] = o_real * c_imag + o_imag * c_real
            for n in range(4):

                @pl.when(chunks[n] == at)
                def _(n=n):
                    store(n).start()
                    store(n + 4).start()

            return carry

        lax.fori_loop(0, depth, backward, 0)

    @pl.when(is_dest & jnp.logical_not(active))
    def _():
        seen[...] = jnp.zeros(seen.shape, F32)
        store_all()

    @pl.when(is_dest)
    def _():
        for n in range(8):
            store(n).wait()


ANY = pl.BlockSpec(memory_space=pl.ANY)
SMEM = pl.BlockSpec(memory_space=pltpu.SMEM)
HALF = jax.ShapeDtypeStruct((2, 2, 128, 256), F32)


def run_main(in_turn, pos_above, pos_below, probe, intensity, table, ins):
    return pl.pallas_call(
        main_kernel,
        out_shape=[pltpu.HBM(HALF.shape, F32)] * 8,
        in_specs=[SMEM] * 3 + [VMEM] * 3 + [ANY] * 8,
        out_specs=[pl.BlockSpec(memory_space=pltpu.HBM)] * 8,
        scratch_shapes=[
            pltpu.VMEM((4, 2, 2, 256, 256), F32),
            pltpu.VMEM((4, 2, 2, 256, 256), F32),
            pltpu.VMEM((2, 256, 256), F32),
            pltpu.SemaphoreType.DMA((2, 8)),
        ],
        compiler_params=pltpu.CompilerParams(vmem_limit_bytes=24 << 20),
        name="probe_chain",
    )(in_turn, pos_above, pos_below, probe, intensity, table, *ins)


VMEM = pl.BlockSpec(memory_space=pltpu.VMEM)
PLANES = 4


def window_offset(positions, slot, tile_at):
    return positions[slot, 0] - 256 * tile_at + 128, positions[slot, 1]


def aligned(row, extent, count):
    return pl.multiple_of(jnp.minimum(row // 8 * 8, extent - count - 8), 8)


def cut_columns(source, first, col, target, count):
    turn = lax.rem(512 - col, 512)
    for at in range(0, count, CHUNK):
        rows = source[pl.ds(first + at, CHUNK), :]
        target[pl.ds(at, CHUNK), :] = pltpu.roll(rows, turn, 1)[:, :256]


def cut_rows(source, first, target):
    start = aligned(first, 256, 128)
    shift = lax.rem(CHUNK + 8 - (first - start), CHUNK + 8)
    for at in range(0, 128, CHUNK):
        target[pl.ds(at, CHUNK), :] = pltpu.roll(source[pl.ds(start + at, CHUNK + 8), :], shift, 0)[:CHUNK]


def cut_all(source, base, positions, pos_above, pos_below, outs, columns):
    out_x, out_y, out_top, out_bottom, out_up, out_down = outs
    depth_at, tile_at, _ = place()
    parity = lax.rem(depth_at, 2)
    col_up = jnp.clip(pos_above[1, 1], 0, 256)
    col_down = jnp.clip(pos_below[0, 1], 0, 256)

    def plane(number, carry):
        part, layer = number // 2, lax.rem(number, 2)
        rows = source.at[part, layer]
        for slot in range(2):
            cut_columns(rows, base, positions[slot, 1], columns.at[slot], 256)
        cut_columns(rows, base, col_up, out_up.at[part, layer], 128)
        cut_columns(rows, base + 128, col_down, out_down.at[part, layer], 128)
        out_top[part, layer] = columns[0, :128]
        out_bottom[part, layer] = columns[1, 128:]
        for slot, out in ((1 - parity, out_x), (parity, out_y)):
            offset = window_offset(positions, slot, tile_at)[0]
            cut_rows(columns.at[slot], offset - 128 * slot, out.at[part, layer])
        return carry

    lax.fori_loop(0, PLANES, plane, 0)


def inner_kernel(positions, strip, out_x, out_y, columns):
    depth_at, tile_at, _ = place()
    parity = lax.rem(depth_at, 2)

    def plane(number, carry):
        part, layer = number // 2, lax.rem(number, 2)
        for slot, out in ((1 - parity, out_x), (parity, out_y)):
            offset, col = window_offset(positions, slot, tile_at)
            cut_columns(strip.at[part, layer], 0, col, columns.at[0], 256)
            cut_rows(columns.at[0], offset - 128 * slot, out.at[part, layer])
        return carry

    lax.fori_loop(0, PLANES, plane, 0)


COLUMNS = pltpu.VMEM((2, 256, 256), F32)


def run_inner(positions, strip):
    return pl.pallas_call(
        inner_kernel,
        out_shape=[HALF] * 2,
        in_specs=[SMEM, VMEM],
        out_specs=[VMEM] * 2,
        scratch_shapes=[COLUMNS],
        compiler_params=pltpu.CompilerParams(vmem_limit_bytes=12 << 20),
        name="cut_inner",
    )(positions, strip)


def wide_halo_kernel(positions, strip, above, below, out_x, out_y, columns):
    depth_at, tile_at, _ = place()
    parity = lax.rem(depth_at, 2)

    def plane(number, carry):
        part, layer = number // 2, lax.rem(number, 2)
        own = strip.at[part, layer]
        for slot, (source, row, own_row) in enumerate(((above, 0, 128), (below, 128, 0))):
            col = positions[slot, 1]
            cut_columns(source.at[part, layer], 0, col, columns.at[slot, pl.ds(row, 128), :], 128)
            cut_columns(own, 128 * slot, col, columns.at[slot, pl.ds(own_row, 128), :], 128)
        for slot, out in ((1 - parity, out_x), (parity, out_y)):
            offset = window_offset(positions, slot, tile_at)[0]
            cut_rows(columns.at[slot], offset - 128 * slot, out.at[part, layer])
        return carry

    lax.fori_loop(0, PLANES, plane, 0)


def run_wide_halo(positions, strip, above, below):
    return pl.pallas_call(
        wide_halo_kernel,
        out_shape=[HALF] * 2,
        in_specs=[SMEM] + [VMEM] * 3,
        out_specs=[VMEM] * 2,
        scratch_shapes=[COLUMNS],
        compiler_params=pltpu.CompilerParams(vmem_limit_bytes=12 << 20),
        name="cut_wide_halo",
    )(positions, strip, above, below)


def halo_kernel(positions, top, bottom, above, below, out_x, out_y, canvas, sems):
    depth_at, tile_at, _ = place()
    copies = [
        pltpu.make_async_copy(source, canvas.at[slot, :, :, pl.ds(row, 128), :], sems.at[number])
        for number, (source, slot, row) in enumerate(((above, 0, 0), (top, 0, 128), (bottom, 1, 0), (below, 1, 128)))
    ]
    for copy in copies:
        copy.start()
    for copy in copies:
        copy.wait()
    parity = lax.rem(depth_at, 2)

    def plane(number, carry):
        part, layer = number // 2, lax.rem(number, 2)
        for slot, out in ((1 - parity, out_x), (parity, out_y)):
            offset = window_offset(positions, slot, tile_at)[0]
            cut_rows(canvas.at[slot, part, layer], offset - 128 * slot, out.at[part, layer])
        return carry

    lax.fori_loop(0, PLANES, plane, 0)


def run_halo(positions, top, bottom, above, below):
    return pl.pallas_call(
        halo_kernel,
        out_shape=[HALF] * 2,
        in_specs=[SMEM] + [ANY] * 4,
        out_specs=[VMEM] * 2,
        scratch_shapes=[pltpu.VMEM((2, 2, 2, 256, 256), F32), pltpu.SemaphoreType.DMA((4,))],
        compiler_params=pltpu.CompilerParams(vmem_limit_bytes=12 << 20),
        name="cut_halo",
    )(positions, top, bottom, above, below)


def by_slot(own, a, b, c, rel):
    first = jnp.where(rel == 0, own, jnp.where(rel == 1, a, jnp.where(rel == 2, c, b)))
    second = jnp.where(rel == 0, a, jnp.where(rel == 1, own, jnp.where(rel == 2, b, c)))
    return first, second


def add_parts(canvas, strip, parts, spots, part, layer):
    for at in range(0, 256, CHUNK):
        canvas[part, layer, pl.ds(128 + at, CHUNK), :] = strip[part, layer, pl.ds(at, CHUNK), :]
    for source, (row, col) in zip(parts, spots):
        start = aligned(row, 512, 128)
        for at in range(0, 128, STEP):
            value = source[part, layer, pl.ds(at, STEP), :] * (-step_rate)
            wide = jnp.concatenate([value, jnp.zeros((8, 256), F32)], axis=0)
            wide = pltpu.roll(wide, row - start, 0)
            wide = jnp.concatenate([wide, jnp.zeros_like(wide)], axis=1)
            spot = (part, layer, pl.ds(start + at, STEP + 8), slice(None))
            canvas[spot] = canvas[spot] + pltpu.roll(wide, col, 1)


def own_kernel(positions, strip, *rest):
    parts, (out, canvas) = rest[:4], rest[4:]
    tile_at = place()[1]
    off_0, col_0 = window_offset(positions, 0, tile_at)
    off_1, col_1 = window_offset(positions, 1, tile_at)
    spots = ((off_0 + 128, col_0), (off_1, col_1), (off_0, col_0), (off_1 + 128, col_1))

    def plane(number, carry):
        part, layer = number // 2, lax.rem(number, 2)
        add_parts(canvas, strip, parts, spots, part, layer)
        out[part, layer] = canvas[part, layer, 128:384]
        return carry

    lax.fori_loop(0, PLANES, plane, 0)


def run_own(positions, strip, parts):
    return pl.pallas_call(
        own_kernel,
        out_shape=jax.ShapeDtypeStruct((2, 2, 256, 512), F32),
        in_specs=[SMEM] + [VMEM] * 5,
        out_specs=VMEM,
        scratch_shapes=[pltpu.VMEM((2, 2, 512, 512), F32)],
        compiler_params=pltpu.CompilerParams(vmem_limit_bytes=16 << 20),
        name="update_own",
    )(positions, strip, *parts)


def edge_kernel(with_cut, positions, pos_above, pos_below, strip, up, down, *rest):
    outs, (canvas, columns, sems) = rest[:-3], rest[-3:]
    tile_at = place()[1]
    off_up, col_up = window_offset(pos_above, 1, tile_at - 1)
    off_down, col_down = window_offset(pos_below, 0, tile_at + 1)
    spots = (
        (jnp.clip(off_up - 128, 0, 128), jnp.clip(col_up, 0, 256)),
        (jnp.clip(off_down, 0, 128) + 256, jnp.clip(col_down, 0, 256)),
    )

    def store(number, part, layer):
        return pltpu.make_async_copy(
            canvas.at[part, layer, pl.ds(128, 256), :], outs[0].at[part, layer], sems.at[number]
        )

    def plane(number, carry):
        part, layer = number // 2, lax.rem(number, 2)
        add_parts(canvas, strip, (up, down), spots, part, layer)
        store(number, part, layer).start()
        return carry

    lax.fori_loop(0, PLANES, plane, 0)
    if with_cut:
        cut_all(canvas, 128, positions, pos_above, pos_below, outs[1:], columns)
    for number in range(PLANES):
        store(number, number // 2, number % 2).wait()


def run_update(with_cut, positions, pos_above, pos_below, strip, up, down):
    return pl.pallas_call(
        functools.partial(edge_kernel, with_cut),
        out_shape=[jax.ShapeDtypeStruct((2, 2, 256, 512), F32)] + [HALF] * (6 * with_cut),
        in_specs=[SMEM] * 3 + [VMEM] * 3,
        out_specs=[ANY] + [VMEM] * (6 * with_cut),
        scratch_shapes=[pltpu.VMEM((2, 2, 512, 512), F32), COLUMNS, pltpu.SemaphoreType.DMA((4,))],
        compiler_params=pltpu.CompilerParams(vmem_limit_bytes=16 << 20),
        name=f"update_{int(with_cut)}",
    )(positions, pos_above, pos_below, strip, up, down)


def pairs(even, odd, tiles):
    return [
        (source * tiles + tile, target * tiles + tile)
        for tile in range(tiles)
        for source, target in (odd if tile % 2 else even)
    ]


def shards(transmission, probe, intensity, positions, batch):
    tiles = lax.axis_size("tile")
    depths = lax.axis_size("depth")
    table = jnp.asarray(operator_table(256))
    flows = [
        pairs([(1, 0), (0, 1)], [(3, 2), (2, 3)], tiles),
        pairs([(3, 0), (2, 1)], [(1, 2), (0, 3)], tiles),
        pairs([(2, 0), (3, 1)], [(0, 2), (1, 3)], tiles),
    ]
    returns = [[(b, a) for a, b in flow] for flow in flows]
    to_next = [(d * tiles + t, d * tiles + t + 1) for d in range(depths) for t in range(tiles - 1)]
    to_last = [(b, a) for a, b in to_next]

    def send(value, flow):
        return lax.ppermute(value, AXES, flow)

    rel = place()[2]
    strip = transmission
    pos_above = send(positions, to_next)
    pos_below = send(positions, to_last)
    for turn_at in range(2):
        if turn_at == 0:
            above = send(strip[:, :, 128:], to_next)
            below = send(strip[:, :, :128], to_last)
            x_inner, y_inner = run_inner(positions, strip)
        else:
            x_inner, y_inner, top, bottom, up, down = cuts
            above = send(down, to_next)
            below = send(up, to_last)
        inner = [y_inner] + [send(v, flow) for v, flow in zip((x_inner, x_inner, y_inner), flows)]
        if turn_at == 0:
            x_halo, y_halo = run_wide_halo(positions, strip, above, below)
        else:
            x_halo, y_halo = run_halo(positions, top, bottom, above, below)
        halo = [y_halo] + [send(v, flow) for v, flow in zip((x_halo, x_halo, y_halo), flows)]
        grads = run_main((batch == turn_at).astype(jnp.int32), pos_above, pos_below, probe, intensity, table, inner + halo)
        halo = [grads[4]] + [send(v, flow) for v, flow in zip(grads[5:], returns)]
        inner = [grads[0]] + [send(v, flow) for v, flow in zip(grads[1:4], returns)]
        to_up, to_down = by_slot(*halo, rel)
        from_below = send(to_up, to_last)
        from_above = send(to_down, to_next)
        strip = run_own(positions, strip, [*by_slot(*inner, rel), to_up, to_down])
        result = run_update(turn_at == 0, positions, pos_above, pos_below, strip, from_above, from_below)
        strip, cuts = result[0], result[1:]
    return strip


def solution(mesh):
    return jax.shard_map(
        shards,
        mesh=mesh,
        in_specs=(
            P(None, "depth", "tile", None),
            P(),
            P("tile", None, None),
            P("tile", None),
            P("tile"),
        ),
        out_specs=P(None, "depth", "tile", None),
        check_vma=False,
    )
```

```python
import functools
import math

import jax
import jax.numpy as jnp
import numpy as np
from jax import lax
from jax.experimental import pallas as pl
from jax.experimental.pallas import tpu as pltpu
from jax.sharding import PartitionSpec as P

prop_strength = 24.0
step_rate = 0.08

AXES = ("depth", "tile")
F32 = jnp.float32
BF16 = jnp.bfloat16
CHUNK = 32
STEP = 64


def operator_table(extent):
    counter = np.arange(extent)
    angles = 2.0 * np.pi / extent * (counter[:, None] * counter[None, :] % extent)
    far = (np.cos(angles) - 1j * np.sin(angles)) / math.sqrt(extent)
    freq = np.where(counter < extent // 2, counter, counter - extent) / extent
    turned = np.exp(-1j * np.pi * prop_strength * freq * freq)
    near = np.conj(far) @ (turned[:, None] * far)
    half = extent // 2
    blocks = [0.5 * (near[:half, :half] + sign * near[:half, half:]) for sign in (1, -1)]
    right = [np.block([[m.real, m.imag], [-m.imag, m.real]]) for m in blocks]
    parts = []
    for value in (*right, far.real, far.imag, far.real + far.imag):
        high = value.astype(BF16)
        low = (value - high.astype(np.float64)).astype(BF16)
        parts += [high, low]
    return np.stack(parts)


def place():
    depth_at = lax.axis_index("depth")
    tile_at = lax.axis_index("tile")
    rel = lax.rem(depth_at + 2 * lax.rem(tile_at, 2), 4)
    return depth_at, tile_at, rel


def split(x):
    high = x.astype(BF16)
    return high, (x - high.astype(F32)).astype(BF16)


def mm(a, b):
    return jnp.dot(a, b, preferred_element_type=F32)


def right_three(x, table, at):
    high, low = split(x)
    lhs = jnp.concatenate([high, high, low], axis=1)
    return mm(lhs, jnp.concatenate([table[at], table[at + 1], table[at]], axis=0))


def crossed(matrix):
    cat = jnp.concatenate
    upper = cat([matrix[:128, :128], matrix[128:, :128]], axis=1)
    return cat([upper, cat([matrix[:128, 128:], matrix[128:, 128:]], axis=1)], axis=0)


def left_three(x, table, at, view=lambda matrix: matrix):
    high, low = split(x)
    upper, lower = view(table[at]), view(table[at + 1])
    lhs = jnp.concatenate([upper, lower, upper], axis=1)
    return mm(lhs, jnp.concatenate([high, high, low], axis=0))


def far_two_sided(x_real, x_imag, table):
    for three in (right_three, left_three):
        first = three(x_real, table, 4)
        second = three(x_imag, table, 6)
        third = three(x_real + x_imag, table, 8)
        x_real, x_imag = first - second, third - first - second
    return x_real, x_imag


def near_two_sided(x_real, x_imag, table):
    cat = jnp.concatenate
    x_a = cat([x_real[:, :128], x_imag[:, :128]], axis=1)
    x_b = cat([x_real[:, 128:], x_imag[:, 128:]], axis=1)
    even, odd = right_three(x_a + x_b, table, 0), right_three(x_a - x_b, table, 2)
    u_a, u_b = even + odd, even - odd
    v_real = cat([u_a[:, :128], u_b[:, :128]], axis=1)
    v_imag = cat([u_a[:, 128:], u_b[:, 128:]], axis=1)
    v_a = cat([v_real[:128], v_imag[:128]], axis=0)
    v_b = cat([v_real[128:], v_imag[128:]], axis=0)
    even, odd = left_three(v_a + v_b, table, 0, crossed), left_three(v_a - v_b, table, 2, crossed)
    y_a, y_b = even + odd, even - odd
    return cat([y_a[:128], y_b[:128]], axis=0), cat([y_a[128:], y_b[128:]], axis=0)


def main_kernel(in_turn, _, __, probe, intensity, table_in, *rest):
    ins, outs, (obj, seen, wave, measured, table, sems) = rest[:8], rest[8:16], rest[16:]
    depth = 4
    depth_at, tile_at, rel = place()
    slot = lax.rem(rel, 2)
    is_dest = rel < 2
    active = is_dest & (in_turn[slot] > 0)
    near = 1 + 2 * slot
    chunks = [depth_at, lax.rem(depth_at + near, 4), lax.rem(depth_at + 4 - near, 4), lax.rem(depth_at + 2, 4)]
    row_inner = pl.multiple_of(128 * (1 - slot), 128)
    row_halo = pl.multiple_of(128 * slot, 128)

    def half(buffer, number):
        row = row_inner if number < 4 else row_halo
        return buffer.at[chunks[number % 4], :, :, pl.ds(row, 128), :]

    def store(n):
        return pltpu.make_async_copy(half(seen, n), outs[n], sems.at[1, n])

    def store_all():
        for n in range(8):
            store(n).start()

    @pl.when(active)
    def _():
        first = pltpu.make_async_copy(probe, wave, sems.at[2, 0])
        tables = pltpu.make_async_copy(table_in, table, sems.at[2, 1])
        level = pltpu.make_async_copy(intensity.at[slot], measured, sems.at[2, 2])
        first.start()
        tables.start()
        for n in range(8):
            pltpu.make_async_copy(ins[n], half(obj, n), sems.at[0, 2 * chunks[n % 4] + n // 4]).start()
        level.start()
        first.wait()
        tables.wait()

        def forward(at, carry):
            for n in range(2):
                pltpu.make_async_copy(ins[4 * n], half(obj, 4 * n), sems.at[0, 2 * at + n]).wait()
            for s in range(2):
                w_real, w_imag = wave[0], wave[1]
                seen[at, 0, s] = w_real
                seen[at, 1, s] = w_imag
                o_real, o_imag = obj[at, 0, s], obj[at, 1, s]
                wave[0], wave[1] = near_two_sided(
                    o_real * w_real - o_imag * w_imag, o_real * w_imag + o_imag * w_real, table
                )
            return carry

        lax.fori_loop(0, depth, forward, 0)
        level.wait()
        f_real, f_imag = far_two_sided(wave[0], wave[1], table)
        factor = 4.0 * (f_real * f_real + f_imag * f_imag - measured[...])
        wave[0], wave[1] = far_two_sided(factor * f_real, -(factor * f_imag), table)

        def backward(step, carry):
            at = depth - 1 - step
            for s in (1, 0):
                c_real, c_imag = near_two_sided(wave[0], wave[1], table)
                s_real, s_imag = seen[at, 0, s], seen[at, 1, s]
                seen[at, 0, s] = c_real * s_real - c_imag * s_imag
                seen[at, 1, s] = -(c_imag * s_real + c_real * s_imag)
                o_real, o_imag = obj[at, 0, s], obj[at, 1, s]
                wave[0] = o_real * c_real - o_imag * c_imag
                wave[1] = o_real * c_imag + o_imag * c_real
            for n in range(4):

                @pl.when(chunks[n] == at)
                def _(n=n):
                    store(n).start()
                    store(n + 4).start()

            return carry

        lax.fori_loop(0, depth, backward, 0)

    @pl.when(is_dest & jnp.logical_not(active))
    def _():
        seen[...] = jnp.zeros(seen.shape, F32)
        store_all()

    @pl.when(is_dest)
    def _():
        for n in range(8):
            store(n).wait()


ANY = pl.BlockSpec(memory_space=pl.ANY)
SMEM = pl.BlockSpec(memory_space=pltpu.SMEM)
HALF = jax.ShapeDtypeStruct((2, 2, 128, 256), F32)


def run_main(in_turn, pos_above, pos_below, probe, intensity, table, ins):
    return pl.pallas_call(
        main_kernel,
        out_shape=[pltpu.HBM(HALF.shape, F32)] * 8,
        in_specs=[SMEM] * 3 + [ANY] * 11,
        out_specs=[pl.BlockSpec(memory_space=pltpu.HBM)] * 8,
        scratch_shapes=[
            pltpu.VMEM((4, 2, 2, 256, 256), F32),
            pltpu.VMEM((4, 2, 2, 256, 256), F32),
            pltpu.VMEM((2, 256, 256), F32),
            pltpu.VMEM((256, 256), F32),
            pltpu.VMEM((10, 256, 256), BF16),
            pltpu.SemaphoreType.DMA((3, 8)),
        ],
        compiler_params=pltpu.CompilerParams(vmem_limit_bytes=24 << 20),
        name="probe_chain",
    )(in_turn, pos_above, pos_below, probe, intensity, table, *ins)


VMEM = pl.BlockSpec(memory_space=pltpu.VMEM)
PLANES = 4


def window_offset(positions, slot, tile_at):
    return positions[slot, 0] - 256 * tile_at + 128, positions[slot, 1]


def aligned(row, extent, count):
    return pl.multiple_of(jnp.minimum(row // 8 * 8, extent - count - 8), 8)


def cut_columns(source, first, col, target, count):
    turn = lax.rem(512 - col, 512)
    for at in range(0, count, CHUNK):
        rows = source[pl.ds(first + at, CHUNK), :]
        target[pl.ds(at, CHUNK), :] = pltpu.roll(rows, turn, 1)[:, :256]


def cut_rows(source, first, target):
    start = aligned(first, 256, 128)
    shift = lax.rem(CHUNK + 8 - (first - start), CHUNK + 8)
    for at in range(0, 128, CHUNK):
        target[pl.ds(at, CHUNK), :] = pltpu.roll(source[pl.ds(start + at, CHUNK + 8), :], shift, 0)[:CHUNK]


def cut_all(source, base, positions, pos_above, pos_below, outs, columns):
    out_x, out_y, out_top, out_bottom, out_up, out_down = outs
    depth_at, tile_at, _ = place()
    parity = lax.rem(depth_at, 2)
    col_up = jnp.clip(pos_above[1, 1], 0, 256)
    col_down = jnp.clip(pos_below[0, 1], 0, 256)

    def plane(number, carry):
        part, layer = number // 2, lax.rem(number, 2)
        rows = source.at[part, layer]
        for slot in range(2):
            cut_columns(rows, base, positions[slot, 1], columns.at[slot], 256)
        cut_columns(rows, base, col_up, out_up.at[part, layer], 128)
        cut_columns(rows, base + 128, col_down, out_down.at[part, layer], 128)
        out_top[part, layer] = columns[0, :128]
        out_bottom[part, layer] = columns[1, 128:]
        for slot, out in ((1 - parity, out_x), (parity, out_y)):
            offset = window_offset(positions, slot, tile_at)[0]
            cut_rows(columns.at[slot], offset - 128 * slot, out.at[part, layer])
        return carry

    lax.fori_loop(0, PLANES, plane, 0)


def inner_kernel(positions, strip, out_x, out_y, columns):
    depth_at, tile_at, _ = place()
    parity = lax.rem(depth_at, 2)

    def plane(number, carry):
        part, layer = number // 2, lax.rem(number, 2)
        for slot, out in ((1 - parity, out_x), (parity, out_y)):
            offset, col = window_offset(positions, slot, tile_at)
            cut_columns(strip.at[part, layer], 0, col, columns.at[0], 256)
            cut_rows(columns.at[0], offset - 128 * slot, out.at[part, layer])
        return carry

    lax.fori_loop(0, PLANES, plane, 0)


COLUMNS = pltpu.VMEM((2, 256, 256), F32)


def run_inner(positions, strip):
    return pl.pallas_call(
        inner_kernel,
        out_shape=[HALF] * 2,
        in_specs=[SMEM, VMEM],
        out_specs=[VMEM] * 2,
        scratch_shapes=[COLUMNS],
        compiler_params=pltpu.CompilerParams(vmem_limit_bytes=12 << 20),
        name="cut_inner",
    )(positions, strip)


def wide_halo_kernel(positions, strip, above, below, out_x, out_y, columns):
    depth_at, tile_at, _ = place()
    parity = lax.rem(depth_at, 2)

    def plane(number, carry):
        part, layer = number // 2, lax.rem(number, 2)
        own = strip.at[part, layer]
        for slot, (source, row, own_row) in enumerate(((above, 0, 128), (below, 128, 0))):
            col = positions[slot, 1]
            cut_columns(source.at[part, layer], 0, col, columns.at[slot, pl.ds(row, 128), :], 128)
            cut_columns(own, 128 * slot, col, columns.at[slot, pl.ds(own_row, 128), :], 128)
        for slot, out in ((1 - parity, out_x), (parity, out_y)):
            offset = window_offset(positions, slot, tile_at)[0]
            cut_rows(columns.at[slot], offset - 128 * slot, out.at[part, layer])
        return carry

    lax.fori_loop(0, PLANES, plane, 0)


def run_wide_halo(positions, strip, above, below):
    return pl.pallas_call(
        wide_halo_kernel,
        out_shape=[HALF] * 2,
        in_specs=[SMEM] + [VMEM] * 3,
        out_specs=[VMEM] * 2,
        scratch_shapes=[COLUMNS],
        compiler_params=pltpu.CompilerParams(vmem_limit_bytes=12 << 20),
        name="cut_wide_halo",
    )(positions, strip, above, below)


def halo_kernel(positions, top, bottom, above, below, out_x, out_y, canvas, sems):
    depth_at, tile_at, _ = place()
    copies = [
        pltpu.make_async_copy(source, canvas.at[slot, :, :, pl.ds(row, 128), :], sems.at[number])
        for number, (source, slot, row) in enumerate(((above, 0, 0), (top, 0, 128), (bottom, 1, 0), (below, 1, 128)))
    ]
    for copy in copies:
        copy.start()
    for copy in copies:
        copy.wait()
    parity = lax.rem(depth_at, 2)

    def plane(number, carry):
        part, layer = number // 2, lax.rem(number, 2)
        for slot, out in ((1 - parity, out_x), (parity, out_y)):
            offset = window_offset(positions, slot, tile_at)[0]
            cut_rows(canvas.at[slot, part, layer], offset - 128 * slot, out.at[part, layer])
        return carry

    lax.fori_loop(0, PLANES, plane, 0)


def run_halo(positions, top, bottom, above, below):
    return pl.pallas_call(
        halo_kernel,
        out_shape=[HALF] * 2,
        in_specs=[SMEM] + [ANY] * 4,
        out_specs=[VMEM] * 2,
        scratch_shapes=[pltpu.VMEM((2, 2, 2, 256, 256), F32), pltpu.SemaphoreType.DMA((4,))],
        compiler_params=pltpu.CompilerParams(vmem_limit_bytes=12 << 20),
        name="cut_halo",
    )(positions, top, bottom, above, below)


def by_slot(own, a, b, c, rel):
    first = jnp.where(rel == 0, own, jnp.where(rel == 1, a, jnp.where(rel == 2, c, b)))
    second = jnp.where(rel == 0, a, jnp.where(rel == 1, own, jnp.where(rel == 2, b, c)))
    return first, second


def add_parts(canvas, strip, parts, spots, part, layer):
    for at in range(0, 256, CHUNK):
        canvas[part, layer, pl.ds(128 + at, CHUNK), :] = strip[part, layer, pl.ds(at, CHUNK), :]
    for source, (row, col) in zip(parts, spots):
        start = aligned(row, 512, 128)
        for at in range(0, 128, STEP):
            value = source[part, layer, pl.ds(at, STEP), :] * (-step_rate)
            wide = jnp.concatenate([value, jnp.zeros((8, 256), F32)], axis=0)
            wide = pltpu.roll(wide, row - start, 0)
            wide = jnp.concatenate([wide, jnp.zeros_like(wide)], axis=1)
            spot = (part, layer, pl.ds(start + at, STEP + 8), slice(None))
            canvas[spot] = canvas[spot] + pltpu.roll(wide, col, 1)


def own_kernel(positions, strip, *rest):
    parts, (out, canvas) = rest[:4], rest[4:]
    tile_at = place()[1]
    off_0, col_0 = window_offset(positions, 0, tile_at)
    off_1, col_1 = window_offset(positions, 1, tile_at)
    spots = ((off_0 + 128, col_0), (off_1, col_1), (off_0, col_0), (off_1 + 128, col_1))

    def plane(number, carry):
        part, layer = number // 2, lax.rem(number, 2)
        add_parts(canvas, strip, parts, spots, part, layer)
        out[part, layer] = canvas[part, layer, 128:384]
        return carry

    lax.fori_loop(0, PLANES, plane, 0)


def run_own(positions, strip, parts):
    return pl.pallas_call(
        own_kernel,
        out_shape=jax.ShapeDtypeStruct((2, 2, 256, 512), F32),
        in_specs=[SMEM] + [VMEM] * 5,
        out_specs=VMEM,
        scratch_shapes=[pltpu.VMEM((2, 2, 512, 512), F32)],
        compiler_params=pltpu.CompilerParams(vmem_limit_bytes=16 << 20),
        name="update_own",
    )(positions, strip, *parts)


def edge_kernel(with_cut, positions, pos_above, pos_below, strip, up, down, *rest):
    outs, (canvas, columns, sems) = rest[:-3], rest[-3:]
    tile_at = place()[1]
    off_up, col_up = window_offset(pos_above, 1, tile_at - 1)
    off_down, col_down = window_offset(pos_below, 0, tile_at + 1)
    spots = (
        (jnp.clip(off_up - 128, 0, 128), jnp.clip(col_up, 0, 256)),
        (jnp.clip(off_down, 0, 128) + 256, jnp.clip(col_down, 0, 256)),
    )

    def store(number, part, layer):
        return pltpu.make_async_copy(
            canvas.at[part, layer, pl.ds(128, 256), :], outs[0].at[part, layer], sems.at[number]
        )

    def plane(number, carry):
        part, layer = number // 2, lax.rem(number, 2)
        add_parts(canvas, strip, (up, down), spots, part, layer)
        store(number, part, layer).start()
        return carry

    lax.fori_loop(0, PLANES, plane, 0)
    if with_cut:
        cut_all(canvas, 128, positions, pos_above, pos_below, outs[1:], columns)
    for number in range(PLANES):
        store(number, number // 2, number % 2).wait()


def run_update(with_cut, positions, pos_above, pos_below, strip, up, down):
    return pl.pallas_call(
        functools.partial(edge_kernel, with_cut),
        out_shape=[jax.ShapeDtypeStruct((2, 2, 256, 512), F32)] + [HALF] * (6 * with_cut),
        in_specs=[SMEM] * 3 + [VMEM] * 3,
        out_specs=[ANY] + [VMEM] * (6 * with_cut),
        scratch_shapes=[pltpu.VMEM((2, 2, 512, 512), F32), COLUMNS, pltpu.SemaphoreType.DMA((4,))],
        compiler_params=pltpu.CompilerParams(vmem_limit_bytes=16 << 20),
        name=f"update_{int(with_cut)}",
    )(positions, pos_above, pos_below, strip, up, down)


def pairs(even, odd, tiles):
    return [
        (source * tiles + tile, target * tiles + tile)
        for tile in range(tiles)
        for source, target in (odd if tile % 2 else even)
    ]


def shards(transmission, probe, intensity, positions, batch):
    tiles = lax.axis_size("tile")
    depths = lax.axis_size("depth")
    table = jnp.asarray(operator_table(256))
    flows = [
        pairs([(1, 0), (0, 1)], [(3, 2), (2, 3)], tiles),
        pairs([(3, 0), (2, 1)], [(1, 2), (0, 3)], tiles),
        pairs([(2, 0), (3, 1)], [(0, 2), (1, 3)], tiles),
    ]
    returns = [[(b, a) for a, b in flow] for flow in flows]
    to_next = [(d * tiles + t, d * tiles + t + 1) for d in range(depths) for t in range(tiles - 1)]
    to_last = [(b, a) for a, b in to_next]

    def send(value, flow):
        return lax.ppermute(value, AXES, flow)

    rel = place()[2]
    strip = transmission
    pos_above = send(positions, to_next)
    pos_below = send(positions, to_last)
    for turn_at in range(2):
        if turn_at == 0:
            above = send(strip[:, :, 128:], to_next)
            below = send(strip[:, :, :128], to_last)
            x_inner, y_inner = run_inner(positions, strip)
        else:
            x_inner, y_inner, top, bottom, up, down = cuts
            above = send(down, to_next)
            below = send(up, to_last)
        inner = [y_inner] + [send(v, flow) for v, flow in zip((x_inner, x_inner, y_inner), flows)]
        if turn_at == 0:
            x_halo, y_halo = run_wide_halo(positions, strip, above, below)
        else:
            x_halo, y_halo = run_halo(positions, top, bottom, above, below)
        halo = [y_halo] + [send(v, flow) for v, flow in zip((x_halo, x_halo, y_halo), flows)]
        grads = run_main((batch == turn_at).astype(jnp.int32), pos_above, pos_below, probe, intensity, table, inner + halo)
        halo = [grads[4]] + [send(v, flow) for v, flow in zip(grads[5:], returns)]
        inner = [grads[0]] + [send(v, flow) for v, flow in zip(grads[1:4], returns)]
        to_up, to_down = by_slot(*halo, rel)
        from_below = send(to_up, to_last)
        from_above = send(to_down, to_next)
        strip = run_own(positions, strip, [*by_slot(*inner, rel), to_up, to_down])
        result = run_update(turn_at == 0, positions, pos_above, pos_below, strip, from_above, from_below)
        strip, cuts = result[0], result[1:]
    return strip


def solution(mesh):
    return jax.shard_map(
        shards,
        mesh=mesh,
        in_specs=(
            P(None, "depth", "tile", None),
            P(),
            P("tile", None, None),
            P("tile", None),
            P("tile"),
        ),
        out_specs=P(None, "depth", "tile", None),
        check_vma=False,
    )
```

```python
import functools
import math

import jax
import jax.numpy as jnp
import numpy as np
from jax import lax
from jax.experimental import pallas as pl
from jax.experimental.pallas import tpu as pltpu
from jax.sharding import PartitionSpec as P

prop_strength = 24.0
step_rate = 0.08

AXES = ("depth", "tile")
F32 = jnp.float32
BF16 = jnp.bfloat16
CHUNK = 32
STEP = 64


def operator_table(extent):
    counter = np.arange(extent)
    angles = 2.0 * np.pi / extent * (counter[:, None] * counter[None, :] % extent)
    far = (np.cos(angles) - 1j * np.sin(angles)) / math.sqrt(extent)
    freq = np.where(counter < extent // 2, counter, counter - extent) / extent
    turned = np.exp(-1j * np.pi * prop_strength * freq * freq)
    near = np.conj(far) @ (turned[:, None] * far)
    half = extent // 2
    blocks = [0.5 * (near[:half, :half] + sign * near[:half, half:]) for sign in (1, -1)]
    right = [np.block([[m.real, m.imag], [-m.imag, m.real]]) for m in blocks]
    parts = []
    for value in (*right, far.real, far.imag, far.real + far.imag):
        high = value.astype(BF16)
        low = (value - high.astype(np.float64)).astype(BF16)
        parts += [high, low]
    return np.stack(parts)


def place():
    depth_at = lax.axis_index("depth")
    tile_at = lax.axis_index("tile")
    rel = lax.rem(depth_at + 2 * lax.rem(tile_at, 2), 4)
    return depth_at, tile_at, rel


def split(x):
    high = x.astype(BF16)
    return high, (x - high.astype(F32)).astype(BF16)


def mm(a, b):
    return jnp.dot(a, b, preferred_element_type=F32)


def right_three(x, table, at):
    high, low = split(x)
    lhs = jnp.concatenate([high, high, low], axis=1)
    return mm(lhs, jnp.concatenate([table[at], table[at + 1], table[at]], axis=0))


def crossed(matrix):
    cat = jnp.concatenate
    upper = cat([matrix[:128, :128], matrix[128:, :128]], axis=1)
    return cat([upper, cat([matrix[:128, 128:], matrix[128:, 128:]], axis=1)], axis=0)


def left_three(x, table, at, view=lambda matrix: matrix):
    high, low = split(x)
    upper, lower = view(table[at]), view(table[at + 1])
    lhs = jnp.concatenate([upper, lower, upper], axis=1)
    return mm(lhs, jnp.concatenate([high, high, low], axis=0))


def far_two_sided(x_real, x_imag, table):
    for three in (right_three, left_three):
        first = three(x_real, table, 4)
        second = three(x_imag, table, 6)
        third = three(x_real + x_imag, table, 8)
        x_real, x_imag = first - second, third - first - second
    return x_real, x_imag


def near_two_sided(x_real, x_imag, table):
    cat = jnp.concatenate
    x_a = cat([x_real[:, :128], x_imag[:, :128]], axis=1)
    x_b = cat([x_real[:, 128:], x_imag[:, 128:]], axis=1)
    even, odd = right_three(x_a + x_b, table, 0), right_three(x_a - x_b, table, 2)
    u_a, u_b = even + odd, even - odd
    v_real = cat([u_a[:, :128], u_b[:, :128]], axis=1)
    v_imag = cat([u_a[:, 128:], u_b[:, 128:]], axis=1)
    v_a = cat([v_real[:128], v_imag[:128]], axis=0)
    v_b = cat([v_real[128:], v_imag[128:]], axis=0)
    even, odd = left_three(v_a + v_b, table, 0, crossed), left_three(v_a - v_b, table, 2, crossed)
    y_a, y_b = even + odd, even - odd
    return cat([y_a[:128], y_b[:128]], axis=0), cat([y_a[128:], y_b[128:]], axis=0)


def main_kernel(in_turn, _, __, probe, intensity, table_in, *rest):
    ins, outs, (obj, seen, wave, measured, table, sems) = rest[:8], rest[8:16], rest[16:]
    depth = 4
    depth_at, tile_at, rel = place()
    slot = lax.rem(rel, 2)
    is_dest = rel < 2
    active = is_dest & (in_turn[slot] > 0)
    near = 1 + 2 * slot
    chunks = [depth_at, lax.rem(depth_at + near, 4), lax.rem(depth_at + 4 - near, 4), lax.rem(depth_at + 2, 4)]
    row_inner = pl.multiple_of(128 * (1 - slot), 128)
    row_halo = pl.multiple_of(128 * slot, 128)

    def half(buffer, number):
        row = row_inner if number < 4 else row_halo
        return buffer.at[chunks[number % 4], :, :, pl.ds(row, 128), :]

    def store(n):
        return pltpu.make_async_copy(half(seen, n), outs[n], sems.at[1, n])

    def store_all():
        for n in range(8):
            store(n).start()

    @pl.when(active)
    def _():
        first = pltpu.make_async_copy(probe, wave, sems.at[2, 0])
        tables = pltpu.make_async_copy(table_in, table, sems.at[2, 1])
        level = pltpu.make_async_copy(intensity.at[slot], measured, sems.at[2, 2])
        first.start()
        tables.start()
        for n in range(8):
            pltpu.make_async_copy(ins[n], half(obj, n), sems.at[0, 2 * chunks[n % 4] + n // 4]).start()
        level.start()
        first.wait()
        tables.wait()

        def forward(at, carry):
            for n in range(2):
                pltpu.make_async_copy(ins[4 * n], half(obj, 4 * n), sems.at[0, 2 * at + n]).wait()
            for s in range(2):
                w_real, w_imag = wave[0], wave[1]
                seen[at, 0, s] = w_real
                seen[at, 1, s] = w_imag
                o_real, o_imag = obj[at, 0, s], obj[at, 1, s]
                wave[0], wave[1] = near_two_sided(
                    o_real * w_real - o_imag * w_imag, o_real * w_imag + o_imag * w_real, table
                )
            return carry

        lax.fori_loop(0, depth, forward, 0)
        level.wait()
        f_real, f_imag = far_two_sided(wave[0], wave[1], table)
        factor = 4.0 * (f_real * f_real + f_imag * f_imag - measured[...])
        wave[0], wave[1] = far_two_sided(factor * f_real, -(factor * f_imag), table)

        def backward(step, carry):
            at = depth - 1 - step
            for s in (1, 0):
                c_real, c_imag = near_two_sided(wave[0], wave[1], table)
                s_real, s_imag = seen[at, 0, s], seen[at, 1, s]
                seen[at, 0, s] = c_real * s_real - c_imag * s_imag
                seen[at, 1, s] = -(c_imag * s_real + c_real * s_imag)
                o_real, o_imag = obj[at, 0, s], obj[at, 1, s]
                wave[0] = o_real * c_real - o_imag * c_imag
                wave[1] = o_real * c_imag + o_imag * c_real
            for n in range(4):

                @pl.when(chunks[n] == at)
                def _(n=n):
                    store(n).start()
                    store(n + 4).start()

            return carry

        lax.fori_loop(0, depth, backward, 0)

    @pl.when(is_dest & jnp.logical_not(active))
    def _():
        seen[...] = jnp.zeros(seen.shape, F32)
        store_all()

    @pl.when(is_dest)
    def _():
        for n in range(8):
            store(n).wait()


ANY = pl.BlockSpec(memory_space=pl.ANY)
SMEM = pl.BlockSpec(memory_space=pltpu.SMEM)
HALF = jax.ShapeDtypeStruct((2, 2, 128, 256), F32)


def run_main(in_turn, pos_above, pos_below, probe, intensity, table, ins):
    return pl.pallas_call(
        main_kernel,
        out_shape=[pltpu.HBM(HALF.shape, F32)] * 8,
        in_specs=[SMEM] * 3 + [ANY] * 11,
        out_specs=[pl.BlockSpec(memory_space=pltpu.HBM)] * 8,
        scratch_shapes=[
            pltpu.VMEM((4, 2, 2, 256, 256), F32),
            pltpu.VMEM((4, 2, 2, 256, 256), F32),
            pltpu.VMEM((2, 256, 256), F32),
            pltpu.VMEM((256, 256), F32),
            pltpu.VMEM((10, 256, 256), BF16),
            pltpu.SemaphoreType.DMA((3, 8)),
        ],
        compiler_params=pltpu.CompilerParams(vmem_limit_bytes=24 << 20),
        name="probe_chain",
    )(in_turn, pos_above, pos_below, probe, intensity, table, *ins)


VMEM = pl.BlockSpec(memory_space=pltpu.VMEM)
PLANES = 4


def window_offset(positions, slot, tile_at):
    return positions[slot, 0] - 256 * tile_at + 128, positions[slot, 1]


def aligned(row, extent, count):
    return pl.multiple_of(jnp.minimum(row // 8 * 8, extent - count - 8), 8)


def cut_columns(source, first, col, target, count):
    turn = lax.rem(512 - col, 512)
    for at in range(0, count, CHUNK):
        rows = source[pl.ds(first + at, CHUNK), :]
        target[pl.ds(at, CHUNK), :] = pltpu.roll(rows, turn, 1)[:, :256]


def cut_rows(source, first, target):
    start = aligned(first, 256, 128)
    shift = lax.rem(CHUNK + 8 - (first - start), CHUNK + 8)
    for at in range(0, 128, CHUNK):
        target[pl.ds(at, CHUNK), :] = pltpu.roll(source[pl.ds(start + at, CHUNK + 8), :], shift, 0)[:CHUNK]


def cut_all(source, base, positions, pos_above, pos_below, outs, columns):
    out_x, out_y, out_top, out_bottom, out_up, out_down = outs
    depth_at, tile_at, _ = place()
    parity = lax.rem(depth_at, 2)
    col_up = jnp.clip(pos_above[1, 1], 0, 256)
    col_down = jnp.clip(pos_below[0, 1], 0, 256)

    def plane(number, carry):
        part, layer = number // 2, lax.rem(number, 2)
        rows = source.at[part, layer]
        for slot in range(2):
            cut_columns(rows, base, positions[slot, 1], columns.at[slot], 256)
        cut_columns(rows, base, col_up, out_up.at[part, layer], 128)
        cut_columns(rows, base + 128, col_down, out_down.at[part, layer], 128)
        out_top[part, layer] = columns[0, :128]
        out_bottom[part, layer] = columns[1, 128:]
        for slot, out in ((1 - parity, out_x), (parity, out_y)):
            offset = window_offset(positions, slot, tile_at)[0]
            cut_rows(columns.at[slot], offset - 128 * slot, out.at[part, layer])
        return carry

    lax.fori_loop(0, PLANES, plane, 0)


def inner_kernel(positions, strip, out_x, out_y, columns):
    depth_at, tile_at, _ = place()
    parity = lax.rem(depth_at, 2)

    def plane(number, carry):
        part, layer = number // 2, lax.rem(number, 2)
        for slot, out in ((1 - parity, out_x), (parity, out_y)):
            offset, col = window_offset(positions, slot, tile_at)
            cut_columns(strip.at[part, layer], 0, col, columns.at[0], 256)
            cut_rows(columns.at[0], offset - 128 * slot, out.at[part, layer])
        return carry

    lax.fori_loop(0, PLANES, plane, 0)


COLUMNS = pltpu.VMEM((2, 256, 256), F32)


def run_inner(positions, strip):
    return pl.pallas_call(
        inner_kernel,
        out_shape=[HALF] * 2,
        in_specs=[SMEM, VMEM],
        out_specs=[VMEM] * 2,
        scratch_shapes=[COLUMNS],
        compiler_params=pltpu.CompilerParams(vmem_limit_bytes=12 << 20),
        name="cut_inner",
    )(positions, strip)


def wide_halo_kernel(positions, strip, above, below, out_x, out_y, columns):
    depth_at, tile_at, _ = place()
    parity = lax.rem(depth_at, 2)

    def plane(number, carry):
        part, layer = number // 2, lax.rem(number, 2)
        own = strip.at[part, layer]
        for slot, (source, row, own_row) in enumerate(((above, 0, 128), (below, 128, 0))):
            col = positions[slot, 1]
            cut_columns(source.at[part, layer], 0, col, columns.at[slot, pl.ds(row, 128), :], 128)
            cut_columns(own, 128 * slot, col, columns.at[slot, pl.ds(own_row, 128), :], 128)
        for slot, out in ((1 - parity, out_x), (parity, out_y)):
            offset = window_offset(positions, slot, tile_at)[0]
            cut_rows(columns.at[slot], offset - 128 * slot, out.at[part, layer])
        return carry

    lax.fori_loop(0, PLANES, plane, 0)


def run_wide_halo(positions, strip, above, below):
    return pl.pallas_call(
        wide_halo_kernel,
        out_shape=[HALF] * 2,
        in_specs=[SMEM] + [VMEM] * 3,
        out_specs=[VMEM] * 2,
        scratch_shapes=[COLUMNS],
        compiler_params=pltpu.CompilerParams(vmem_limit_bytes=12 << 20),
        name="cut_wide_halo",
    )(positions, strip, above, below)


def halo_kernel(positions, top, bottom, above, below, out_x, out_y, canvas, sems):
    depth_at, tile_at, _ = place()
    copies = [
        pltpu.make_async_copy(source, canvas.at[slot, :, :, pl.ds(row, 128), :], sems.at[number])
        for number, (source, slot, row) in enumerate(((above, 0, 0), (top, 0, 128), (bottom, 1, 0), (below, 1, 128)))
    ]
    for copy in copies:
        copy.start()
    for copy in copies:
        copy.wait()
    parity = lax.rem(depth_at, 2)

    def plane(number, carry):
        part, layer = number // 2, lax.rem(number, 2)
        for slot, out in ((1 - parity, out_x), (parity, out_y)):
            offset = window_offset(positions, slot, tile_at)[0]
            cut_rows(canvas.at[slot, part, layer], offset - 128 * slot, out.at[part, layer])
        return carry

    lax.fori_loop(0, PLANES, plane, 0)


def run_halo(positions, top, bottom, above, below):
    return pl.pallas_call(
        halo_kernel,
        out_shape=[HALF] * 2,
        in_specs=[SMEM] + [ANY] * 4,
        out_specs=[VMEM] * 2,
        scratch_shapes=[pltpu.VMEM((2, 2, 2, 256, 256), F32), pltpu.SemaphoreType.DMA((4,))],
        compiler_params=pltpu.CompilerParams(vmem_limit_bytes=12 << 20),
        name="cut_halo",
    )(positions, top, bottom, above, below)


def by_slot(own, a, b, c, rel):
    first = jnp.where(rel == 0, own, jnp.where(rel == 1, a, jnp.where(rel == 2, c, b)))
    second = jnp.where(rel == 0, a, jnp.where(rel == 1, own, jnp.where(rel == 2, b, c)))
    return first, second


def add_parts(canvas, strip, parts, spots, part, layer):
    for at in range(0, 256, CHUNK):
        canvas[part, layer, pl.ds(128 + at, CHUNK), :] = strip[part, layer, pl.ds(at, CHUNK), :]
    for source, (row, col) in zip(parts, spots):
        start = aligned(row, 512, 128)
        for at in range(0, 128, STEP):
            value = source[part, layer, pl.ds(at, STEP), :] * (-step_rate)
            wide = jnp.concatenate([value, jnp.zeros((8, 256), F32)], axis=0)
            wide = pltpu.roll(wide, row - start, 0)
            wide = jnp.concatenate([wide, jnp.zeros_like(wide)], axis=1)
            spot = (part, layer, pl.ds(start + at, STEP + 8), slice(None))
            canvas[spot] = canvas[spot] + pltpu.roll(wide, col, 1)


def own_kernel(positions, strip, *rest):
    parts, (out, canvas) = rest[:4], rest[4:]
    tile_at = place()[1]
    off_0, col_0 = window_offset(positions, 0, tile_at)
    off_1, col_1 = window_offset(positions, 1, tile_at)
    spots = ((off_0 + 128, col_0), (off_1, col_1), (off_0, col_0), (off_1 + 128, col_1))

    def plane(number, carry):
        part, layer = number // 2, lax.rem(number, 2)
        add_parts(canvas, strip, parts, spots, part, layer)
        out[part, layer] = canvas[part, layer, 128:384]
        return carry

    lax.fori_loop(0, PLANES, plane, 0)


def run_own(positions, strip, parts):
    return pl.pallas_call(
        own_kernel,
        out_shape=jax.ShapeDtypeStruct((2, 2, 256, 512), F32),
        in_specs=[SMEM] + [VMEM] * 5,
        out_specs=VMEM,
        scratch_shapes=[pltpu.VMEM((2, 2, 512, 512), F32)],
        compiler_params=pltpu.CompilerParams(vmem_limit_bytes=16 << 20),
        name="update_own",
    )(positions, strip, *parts)


def edge_kernel(with_cut, positions, pos_above, pos_below, strip, up, down, *rest):
    outs, (canvas, columns, sems) = rest[:-3], rest[-3:]
    tile_at = place()[1]
    off_up, col_up = window_offset(pos_above, 1, tile_at - 1)
    off_down, col_down = window_offset(pos_below, 0, tile_at + 1)
    spots = (
        (jnp.clip(off_up - 128, 0, 128), jnp.clip(col_up, 0, 256)),
        (jnp.clip(off_down, 0, 128) + 256, jnp.clip(col_down, 0, 256)),
    )

    def store(number, part, layer):
        return pltpu.make_async_copy(
            canvas.at[part, layer, pl.ds(128, 256), :], outs[0].at[part, layer], sems.at[number]
        )

    def plane(number, carry):
        part, layer = number // 2, lax.rem(number, 2)
        add_parts(canvas, strip, (up, down), spots, part, layer)
        store(number, part, layer).start()
        return carry

    lax.fori_loop(0, PLANES, plane, 0)
    if with_cut:
        cut_all(canvas, 128, positions, pos_above, pos_below, outs[1:], columns)
    for number in range(PLANES):
        store(number, number // 2, number % 2).wait()


def run_update(with_cut, positions, pos_above, pos_below, strip, up, down):
    return pl.pallas_call(
        functools.partial(edge_kernel, with_cut),
        out_shape=[jax.ShapeDtypeStruct((2, 2, 256, 512), F32)] + [HALF] * (6 * with_cut),
        in_specs=[SMEM] * 3 + [VMEM] * 3,
        out_specs=[ANY] + [VMEM] * (6 * with_cut),
        scratch_shapes=[pltpu.VMEM((2, 2, 512, 512), F32), COLUMNS, pltpu.SemaphoreType.DMA((4,))],
        compiler_params=pltpu.CompilerParams(vmem_limit_bytes=16 << 20),
        name=f"update_{int(with_cut)}",
    )(positions, pos_above, pos_below, strip, up, down)


def pairs(even, odd, tiles):
    return [
        (source * tiles + tile, target * tiles + tile)
        for tile in range(tiles)
        for source, target in (odd if tile % 2 else even)
    ]


def shards(transmission, probe, intensity, positions, batch):
    tiles = lax.axis_size("tile")
    depths = lax.axis_size("depth")
    table = jnp.asarray(operator_table(256))
    flows = [
        pairs([(1, 0), (0, 1)], [(3, 2), (2, 3)], tiles),
        pairs([(3, 0), (2, 1)], [(1, 2), (0, 3)], tiles),
        pairs([(2, 0), (3, 1)], [(0, 2), (1, 3)], tiles),
    ]
    returns = [[(b, a) for a, b in flow] for flow in flows]
    inside = [(d * tiles + t, d * tiles + (t ^ 1)) for d in range(depths) for t in range(tiles)]
    across = [(d * tiles + t, d * tiles + ((t + 1) ^ 1) - 1) for d in range(depths) for t in range(1, tiles - 1)]

    def send(value, flow):
        return lax.ppermute(value, AXES, flow)

    def exchange(up, down):
        even = lax.rem(lax.axis_index("tile"), 2) == 0
        near = send(jnp.where(even, down, up), inside)
        far = send(jnp.where(even, up, down), across)
        return jnp.where(even, far, near), jnp.where(even, near, far)

    rel = place()[2]
    strip = transmission
    pos_above, pos_below = exchange(positions, positions)
    for turn_at in range(2):
        if turn_at == 0:
            above, below = exchange(strip[:, :, :128], strip[:, :, 128:])
            x_inner, y_inner = run_inner(positions, strip)
        else:
            x_inner, y_inner, top, bottom, up, down = cuts
            above, below = exchange(up, down)
        inner = [y_inner] + [send(v, flow) for v, flow in zip((x_inner, x_inner, y_inner), flows)]
        if turn_at == 0:
            x_halo, y_halo = run_wide_halo(positions, strip, above, below)
        else:
            x_halo, y_halo = run_halo(positions, top, bottom, above, below)
        halo = [y_halo] + [send(v, flow) for v, flow in zip((x_halo, x_halo, y_halo), flows)]
        grads = run_main((batch == turn_at).astype(jnp.int32), pos_above, pos_below, probe, intensity, table, inner + halo)
        halo = [grads[4]] + [send(v, flow) for v, flow in zip(grads[5:], returns)]
        inner = [grads[0]] + [send(v, flow) for v, flow in zip(grads[1:4], returns)]
        to_up, to_down = by_slot(*halo, rel)
        from_above, from_below = exchange(to_up, to_down)
        strip = run_own(positions, strip, [*by_slot(*inner, rel), to_up, to_down])
        result = run_update(turn_at == 0, positions, pos_above, pos_below, strip, from_above, from_below)
        strip, cuts = result[0], result[1:]
    return strip


def solution(mesh):
    return jax.shard_map(
        shards,
        mesh=mesh,
        in_specs=(
            P(None, "depth", "tile", None),
            P(),
            P("tile", None, None),
            P("tile", None),
            P("tile"),
        ),
        out_specs=P(None, "depth", "tile", None),
        check_vma=False,
    )
```

```python
import functools
import math

import jax
import jax.numpy as jnp
import numpy as np
from jax import lax
from jax.experimental import pallas as pl
from jax.experimental.pallas import tpu as pltpu
from jax.sharding import PartitionSpec as P


prop_strength = 24.0
step_rate = 0.08

AXES = ("depth", "tile")
F32 = jnp.float32
BF16 = jnp.bfloat16
CHUNK = 32
STEP = 64


def operator_table(extent):
    counter = np.arange(extent)
    angles = 2.0 * np.pi / extent * (counter[:, None] * counter[None, :] % extent)
    far = (np.cos(angles) - 1j * np.sin(angles)) / math.sqrt(extent)
    freq = np.where(counter < extent // 2, counter, counter - extent) / extent
    turned = np.exp(-1j * np.pi * prop_strength * freq * freq)
    near = np.conj(far) @ (turned[:, None] * far)
    half = extent // 2
    blocks = [0.5 * (near[:half, :half] + sign * near[:half, half:]) for sign in (1, -1)]
    right = [np.block([[m.real, m.imag], [-m.imag, m.real]]) for m in blocks]
    parts = []
    for value in (*right, far.real, far.imag, far.real + far.imag):
        high = value.astype(BF16)
        low = (value - high.astype(np.float64)).astype(BF16)
        parts += [high, low]
    return np.stack(parts)


def place():
    depth_at = lax.axis_index("depth")
    tile_at = lax.axis_index("tile")
    rel = lax.rem(depth_at + 2 * lax.rem(tile_at, 2), 4)
    return depth_at, tile_at, rel


def split(x):
    high = x.astype(BF16)
    return high, (x - high.astype(F32)).astype(BF16)


def mm(a, b):
    return jnp.dot(a, b, preferred_element_type=F32)


def right_three(x, table, at):
    high, low = split(x)
    lhs = jnp.concatenate([high, high, low], axis=1)
    return mm(lhs, jnp.concatenate([table[at], table[at + 1], table[at]], axis=0))


def crossed(matrix):
    cat = jnp.concatenate
    upper = cat([matrix[:128, :128], matrix[128:, :128]], axis=1)
    return cat([upper, cat([matrix[:128, 128:], matrix[128:, 128:]], axis=1)], axis=0)


def left_three(x, table, at, view=lambda matrix: matrix):
    high, low = split(x)
    upper, lower = view(table[at]), view(table[at + 1])
    lhs = jnp.concatenate([upper, lower, upper], axis=1)
    return mm(lhs, jnp.concatenate([high, high, low], axis=0))


def far_two_sided(x_real, x_imag, table):
    for three in (right_three, left_three):
        first = three(x_real, table, 4)
        second = three(x_imag, table, 6)
        third = three(x_real + x_imag, table, 8)
        x_real, x_imag = first - second, third - first - second
    return x_real, x_imag


def near_two_sided(x_real, x_imag, table):
    cat = jnp.concatenate
    x_a = cat([x_real[:, :128], x_imag[:, :128]], axis=1)
    x_b = cat([x_real[:, 128:], x_imag[:, 128:]], axis=1)
    even, odd = right_three(x_a + x_b, table, 0), right_three(x_a - x_b, table, 2)
    u_a, u_b = even + odd, even - odd
    v_real = cat([u_a[:, :128], u_b[:, :128]], axis=1)
    v_imag = cat([u_a[:, 128:], u_b[:, 128:]], axis=1)
    v_a = cat([v_real[:128], v_imag[:128]], axis=0)
    v_b = cat([v_real[128:], v_imag[128:]], axis=0)
    even, odd = left_three(v_a + v_b, table, 0, crossed), left_three(v_a - v_b, table, 2, crossed)
    y_a, y_b = even + odd, even - odd
    return cat([y_a[:128], y_b[:128]], axis=0), cat([y_a[128:], y_b[128:]], axis=0)


def main_kernel(in_turn, _, __, probe, intensity, table_in, *rest):
    ins, outs, (obj, seen, wave, measured, table, sems) = rest[:8], rest[8:16], rest[16:]
    depth = 4
    depth_at, _, rel = place()
    slot = lax.rem(rel, 2)
    is_dest = rel < 2
    active = is_dest & (in_turn[slot] > 0)
    near = 1 + 2 * slot
    chunks = [depth_at, lax.rem(depth_at + near, 4), lax.rem(depth_at + 4 - near, 4), lax.rem(depth_at + 2, 4)]
    row_inner = pl.multiple_of(128 * (1 - slot), 128)
    row_halo = pl.multiple_of(128 * slot, 128)

    def half(buffer, number):
        row = row_inner if number < 4 else row_halo
        return buffer.at[chunks[number % 4], :, :, pl.ds(row, 128), :]

    def store(n):
        return pltpu.make_async_copy(half(seen, n), outs[n], sems.at[1, n])

    def store_all():
        for n in range(8):
            store(n).start()

    @pl.when(active)
    def _():
        first = pltpu.make_async_copy(probe, wave, sems.at[2, 0])
        tables = pltpu.make_async_copy(table_in, table, sems.at[2, 1])
        level = pltpu.make_async_copy(intensity.at[slot], measured, sems.at[2, 2])
        first.start()
        tables.start()
        for n in range(8):
            pltpu.make_async_copy(ins[n], half(obj, n), sems.at[0, 2 * chunks[n % 4] + n // 4]).start()
        level.start()
        first.wait()
        tables.wait()

        def forward(at, carry):
            for n in range(2):
                pltpu.make_async_copy(ins[4 * n], half(obj, 4 * n), sems.at[0, 2 * at + n]).wait()
            for s in range(2):
                w_real, w_imag = wave[0], wave[1]
                seen[at, 0, s] = w_real
                seen[at, 1, s] = w_imag
                o_real, o_imag = obj[at, 0, s], obj[at, 1, s]
                wave[0], wave[1] = near_two_sided(
                    o_real * w_real - o_imag * w_imag, o_real * w_imag + o_imag * w_real, table
                )
            return carry

        lax.fori_loop(0, depth, forward, 0)
        level.wait()
        f_real, f_imag = far_two_sided(wave[0], wave[1], table)
        factor = 4.0 * (f_real * f_real + f_imag * f_imag - measured[...])
        wave[0], wave[1] = far_two_sided(factor * f_real, -(factor * f_imag), table)

        def backward(step, carry):
            at = depth - 1 - step
            for s in (1, 0):
                c_real, c_imag = near_two_sided(wave[0], wave[1], table)
                s_real, s_imag = seen[at, 0, s], seen[at, 1, s]
                seen[at, 0, s] = c_real * s_real - c_imag * s_imag
                seen[at, 1, s] = -(c_imag * s_real + c_real * s_imag)
                o_real, o_imag = obj[at, 0, s], obj[at, 1, s]
                wave[0] = o_real * c_real - o_imag * c_imag
                wave[1] = o_real * c_imag + o_imag * c_real
            for n in range(4):

                @pl.when(chunks[n] == at)
                def _(n=n):
                    store(n).start()
                    store(n + 4).start()

            return carry

        lax.fori_loop(0, depth, backward, 0)

    @pl.when(is_dest & jnp.logical_not(active))
    def _():
        seen[...] = jnp.zeros(seen.shape, F32)
        store_all()

    @pl.when(is_dest)
    def _():
        for n in range(8):
            store(n).wait()


ANY = pl.BlockSpec(memory_space=pl.ANY)
SMEM = pl.BlockSpec(memory_space=pltpu.SMEM)
HALF = jax.ShapeDtypeStruct((2, 2, 128, 256), F32)


def run_main(in_turn, pos_above, pos_below, probe, intensity, table, ins):
    return pl.pallas_call(
        main_kernel,
        out_shape=[pltpu.HBM(HALF.shape, F32)] * 8,
        in_specs=[SMEM] * 3 + [ANY] * 11,
        out_specs=[pl.BlockSpec(memory_space=pltpu.HBM)] * 8,
        scratch_shapes=[
            pltpu.VMEM((4, 2, 2, 256, 256), F32),
            pltpu.VMEM((4, 2, 2, 256, 256), F32),
            pltpu.VMEM((2, 256, 256), F32),
            pltpu.VMEM((256, 256), F32),
            pltpu.VMEM((10, 256, 256), BF16),
            pltpu.SemaphoreType.DMA((3, 8)),
        ],
        compiler_params=pltpu.CompilerParams(vmem_limit_bytes=24 << 20),
        name="probe_chain",
    )(in_turn, pos_above, pos_below, probe, intensity, table, *ins)


VMEM = pl.BlockSpec(memory_space=pltpu.VMEM)
PLANES = 4


def window_offset(positions, slot, tile_at):
    return positions[slot, 0] - 256 * tile_at + 128, positions[slot, 1]


def aligned(row, extent, count):
    return pl.multiple_of(jnp.minimum(row // 8 * 8, extent - count - 8), 8)


def cut_columns(source, first, col, target, count):
    turn = lax.rem(512 - col, 512)
    for at in range(0, count, CHUNK):
        rows = source[pl.ds(first + at, CHUNK), :]
        target[pl.ds(at, CHUNK), :] = pltpu.roll(rows, turn, 1)[:, :256]


def cut_rows(source, first, target):
    start = aligned(first, 256, 128)
    shift = lax.rem(CHUNK + 8 - (first - start), CHUNK + 8)
    for at in range(0, 128, CHUNK):
        target[pl.ds(at, CHUNK), :] = pltpu.roll(source[pl.ds(start + at, CHUNK + 8), :], shift, 0)[:CHUNK]


def cut_all(source, base, positions, pos_above, pos_below, outs, columns):
    out_x, out_y, out_top, out_bottom, out_up, out_down = outs
    depth_at, tile_at, _ = place()
    parity = lax.rem(depth_at, 2)
    col_up = jnp.clip(pos_above[1, 1], 0, 256)
    col_down = jnp.clip(pos_below[0, 1], 0, 256)

    def plane(number, carry):
        part, layer = number // 2, lax.rem(number, 2)
        rows = source.at[part, layer]
        for slot in range(2):
            cut_columns(rows, base, positions[slot, 1], columns.at[slot], 256)
        cut_columns(rows, base, col_up, out_up.at[part, layer], 128)
        cut_columns(rows, base + 128, col_down, out_down.at[part, layer], 128)
        out_top[part, layer] = columns[0, :128]
        out_bottom[part, layer] = columns[1, 128:]
        for slot, out in ((1 - parity, out_x), (parity, out_y)):
            offset = window_offset(positions, slot, tile_at)[0]
            cut_rows(columns.at[slot], offset - 128 * slot, out.at[part, layer])
        return carry

    lax.fori_loop(0, PLANES, plane, 0)


def inner_kernel(positions, strip, out_x, out_y, columns):
    depth_at, tile_at, _ = place()
    parity = lax.rem(depth_at, 2)

    def plane(number, carry):
        part, layer = number // 2, lax.rem(number, 2)
        for slot, out in ((1 - parity, out_x), (parity, out_y)):
            offset, col = window_offset(positions, slot, tile_at)
            cut_columns(strip.at[part, layer], 0, col, columns.at[0], 256)
            cut_rows(columns.at[0], offset - 128 * slot, out.at[part, layer])
        return carry

    lax.fori_loop(0, PLANES, plane, 0)


COLUMNS = pltpu.VMEM((2, 256, 256), F32)


def run_inner(positions, strip):
    return pl.pallas_call(
        inner_kernel,
        out_shape=[HALF] * 2,
        in_specs=[SMEM, VMEM],
        out_specs=[VMEM] * 2,
        scratch_shapes=[COLUMNS],
        compiler_params=pltpu.CompilerParams(vmem_limit_bytes=12 << 20),
        name="cut_inner",
    )(positions, strip)


def wide_halo_kernel(positions, strip, above, below, out_x, out_y, columns):
    depth_at, tile_at, _ = place()
    parity = lax.rem(depth_at, 2)

    def plane(number, carry):
        part, layer = number // 2, lax.rem(number, 2)
        own = strip.at[part, layer]
        for slot, (source, row, own_row) in enumerate(((above, 0, 128), (below, 128, 0))):
            col = positions[slot, 1]
            cut_columns(source.at[part, layer], 0, col, columns.at[slot, pl.ds(row, 128), :], 128)
            cut_columns(own, 128 * slot, col, columns.at[slot, pl.ds(own_row, 128), :], 128)
        for slot, out in ((1 - parity, out_x), (parity, out_y)):
            offset = window_offset(positions, slot, tile_at)[0]
            cut_rows(columns.at[slot], offset - 128 * slot, out.at[part, layer])
        return carry

    lax.fori_loop(0, PLANES, plane, 0)


def run_wide_halo(positions, strip, above, below):
    return pl.pallas_call(
        wide_halo_kernel,
        out_shape=[HALF] * 2,
        in_specs=[SMEM] + [VMEM] * 3,
        out_specs=[VMEM] * 2,
        scratch_shapes=[COLUMNS],
        compiler_params=pltpu.CompilerParams(vmem_limit_bytes=12 << 20),
        name="cut_wide_halo",
    )(positions, strip, above, below)


def halo_kernel(positions, top, bottom, above, below, out_x, out_y, canvas, sems):
    depth_at, tile_at, _ = place()
    copies = [
        pltpu.make_async_copy(source, canvas.at[slot, :, :, pl.ds(row, 128), :], sems.at[number])
        for number, (source, slot, row) in enumerate(((above, 0, 0), (top, 0, 128), (bottom, 1, 0), (below, 1, 128)))
    ]
    for copy in copies:
        copy.start()
    for copy in copies:
        copy.wait()
    parity = lax.rem(depth_at, 2)

    def plane(number, carry):
        part, layer = number // 2, lax.rem(number, 2)
        for slot, out in ((1 - parity, out_x), (parity, out_y)):
            offset = window_offset(positions, slot, tile_at)[0]
            cut_rows(canvas.at[slot, part, layer], offset - 128 * slot, out.at[part, layer])
        return carry

    lax.fori_loop(0, PLANES, plane, 0)


def run_halo(positions, top, bottom, above, below):
    return pl.pallas_call(
        halo_kernel,
        out_shape=[HALF] * 2,
        in_specs=[SMEM] + [ANY] * 4,
        out_specs=[VMEM] * 2,
        scratch_shapes=[pltpu.VMEM((2, 2, 2, 256, 256), F32), pltpu.SemaphoreType.DMA((4,))],
        compiler_params=pltpu.CompilerParams(vmem_limit_bytes=12 << 20),
        name="cut_halo",
    )(positions, top, bottom, above, below)


def by_slot(own, a, b, c, rel):
    first = jnp.where(rel == 0, own, jnp.where(rel == 1, a, jnp.where(rel == 2, c, b)))
    second = jnp.where(rel == 0, a, jnp.where(rel == 1, own, jnp.where(rel == 2, b, c)))
    return first, second


def add_parts(canvas, strip, parts, spots, part, layer):
    for at in range(0, 256, CHUNK):
        canvas[part, layer, pl.ds(128 + at, CHUNK), :] = strip[part, layer, pl.ds(at, CHUNK), :]
    for source, (row, col) in zip(parts, spots):
        start = aligned(row, 512, 128)
        for at in range(0, 128, STEP):
            value = source[part, layer, pl.ds(at, STEP), :] * (-step_rate)
            wide = jnp.concatenate([value, jnp.zeros((8, 256), F32)], axis=0)
            wide = pltpu.roll(wide, row - start, 0)
            wide = jnp.concatenate([wide, jnp.zeros_like(wide)], axis=1)
            spot = (part, layer, pl.ds(start + at, STEP + 8), slice(None))
            canvas[spot] = canvas[spot] + pltpu.roll(wide, col, 1)


def own_kernel(positions, strip, *rest):
    parts, (out, canvas) = rest[:4], rest[4:]
    tile_at = place()[1]
    off_0, col_0 = window_offset(positions, 0, tile_at)
    off_1, col_1 = window_offset(positions, 1, tile_at)
    spots = ((off_0 + 128, col_0), (off_1, col_1), (off_0, col_0), (off_1 + 128, col_1))

    def plane(number, carry):
        part, layer = number // 2, lax.rem(number, 2)
        add_parts(canvas, strip, parts, spots, part, layer)
        out[part, layer] = canvas[part, layer, 128:384]
        return carry

    lax.fori_loop(0, PLANES, plane, 0)


def run_own(positions, strip, parts):
    return pl.pallas_call(
        own_kernel,
        out_shape=jax.ShapeDtypeStruct((2, 2, 256, 512), F32),
        in_specs=[SMEM] + [VMEM] * 5,
        out_specs=VMEM,
        scratch_shapes=[pltpu.VMEM((2, 2, 512, 512), F32)],
        compiler_params=pltpu.CompilerParams(vmem_limit_bytes=16 << 20),
        name="update_own",
    )(positions, strip, *parts)


def edge_kernel(with_cut, positions, pos_above, pos_below, strip, up, down, *rest):
    outs, (canvas, columns, sems) = rest[:-3], rest[-3:]
    tile_at = place()[1]
    off_up, col_up = window_offset(pos_above, 1, tile_at - 1)
    off_down, col_down = window_offset(pos_below, 0, tile_at + 1)
    spots = (
        (jnp.clip(off_up - 128, 0, 128), jnp.clip(col_up, 0, 256)),
        (jnp.clip(off_down, 0, 128) + 256, jnp.clip(col_down, 0, 256)),
    )

    def store(number, part, layer):
        return pltpu.make_async_copy(
            canvas.at[part, layer, pl.ds(128, 256), :], outs[0].at[part, layer], sems.at[number]
        )

    def plane(number, carry):
        part, layer = number // 2, lax.rem(number, 2)
        add_parts(canvas, strip, (up, down), spots, part, layer)
        store(number, part, layer).start()
        return carry

    lax.fori_loop(0, PLANES, plane, 0)
    if with_cut:
        cut_all(canvas, 128, positions, pos_above, pos_below, outs[1:], columns)
    for number in range(PLANES):
        store(number, number // 2, number % 2).wait()


def run_update(with_cut, positions, pos_above, pos_below, strip, up, down):
    return pl.pallas_call(
        functools.partial(edge_kernel, with_cut),
        out_shape=[jax.ShapeDtypeStruct((2, 2, 256, 512), F32)] + [HALF] * (6 * with_cut),
        in_specs=[SMEM] * 3 + [VMEM] * 3,
        out_specs=[ANY] + [VMEM] * (6 * with_cut),
        scratch_shapes=[pltpu.VMEM((2, 2, 512, 512), F32), COLUMNS, pltpu.SemaphoreType.DMA((4,))],
        compiler_params=pltpu.CompilerParams(vmem_limit_bytes=16 << 20),
    )(positions, pos_above, pos_below, strip, up, down)


def pairs(even, odd, tiles):
    return [
        (source * tiles + tile, target * tiles + tile)
        for tile in range(tiles)
        for source, target in (odd if tile % 2 else even)
    ]


def shards(transmission, probe, intensity, positions, batch):
    tiles = lax.axis_size("tile")
    depths = lax.axis_size("depth")
    table = jnp.asarray(operator_table(256))
    flows = [
        pairs([(1, 0), (0, 1)], [(3, 2), (2, 3)], tiles),
        pairs([(3, 0), (2, 1)], [(1, 2), (0, 3)], tiles),
        pairs([(2, 0), (3, 1)], [(0, 2), (1, 3)], tiles),
    ]
    returns = [[(b, a) for a, b in flow] for flow in flows]
    inside = [(d * tiles + t, d * tiles + (t ^ 1)) for d in range(depths) for t in range(tiles)]
    across = [(d * tiles + t, d * tiles + ((t + 1) ^ 1) - 1) for d in range(depths) for t in range(1, tiles - 1)]

    def send_three(values, along):
        last = send(values[2], along[2])
        return [send(values[0], along[0]), send(values[1], along[1]), last]

    def send(value, flow):
        return lax.ppermute(value, AXES, flow)

    def exchange(up, down):
        even = lax.rem(lax.axis_index("tile"), 2) == 0
        far = send(jnp.where(even, up, down), across)
        near = send(jnp.where(even, down, up), inside)
        return jnp.where(even, far, near), jnp.where(even, near, far)

    rel = place()[2]
    strip = transmission
    pos_above, pos_below = exchange(positions, positions)
    for turn_at in range(2):
        if turn_at == 0:
            above, below = exchange(strip[:, :, :128], strip[:, :, 128:])
            x_inner, y_inner = run_inner(positions, strip)
        else:
            x_inner, y_inner, top, bottom, up, down = cuts
            above, below = exchange(up, down)
        inner = [y_inner] + send_three((x_inner, x_inner, y_inner), flows)
        if turn_at == 0:
            x_halo, y_halo = run_wide_halo(positions, strip, above, below)
        else:
            x_halo, y_halo = run_halo(positions, top, bottom, above, below)
        halo = [y_halo] + send_three((x_halo, x_halo, y_halo), flows)
        grads = run_main((batch == turn_at).astype(jnp.int32), pos_above, pos_below, probe, intensity, table, inner + halo)
        halo = [grads[4]] + send_three(grads[5:], returns)
        inner = [grads[0]] + send_three(grads[1:4], returns)
        to_up, to_down = by_slot(*halo, rel)
        from_above, from_below = exchange(to_up, to_down)
        strip = run_own(positions, strip, [*by_slot(*inner, rel), to_up, to_down])
        result = run_update(turn_at == 0, positions, pos_above, pos_below, strip, from_above, from_below)
        strip, cuts = result[0], result[1:]
    return strip


def solution(mesh):
    return jax.shard_map(
        shards,
        mesh=mesh,
        in_specs=(
            P(None, "depth", "tile", None),
            P(),
            P("tile", None, None),
            P("tile", None),
            P("tile"),
        ),
        out_specs=P(None, "depth", "tile", None),
        check_vma=False,
    )
```
